512 devices in a mesh: depth: 8 (over x, core), lat: 64 (over z, y).
Axes of the slice: x: 4, y: 4, z: 16, core: 2. Of those that a mesh axis runs over, the one named last changes fastest.
Arguments:
- object_field: bfloat16 [2, 64, 8192, 256], P(None, 'depth', 'lat'), may hold values from -6 to 6
- probe_field: bfloat16 [2, 128, 256], replicated, may hold values from -6 to 6
- intensity: bfloat16 [512, 128, 256], P('lat'), may hold values from 0.099609375 to 4
- depth_phase: float32 [32, 64], P(None, 'depth'), may hold values from -3.140625 to 3.140625
- shear_rate: int32 [32], replicated, may hold values from -64 to 64
- positions: int32 [512], P('lat'), may hold values from -32 to 32
- angle_index: int32 [512], P('lat'), may hold values from 0 to 31
- frame_count: int32 [64], P('lat'), may hold values from 1 to 8, 320 in all
Outputs:
- correction: float32 [2, 64, 8192, 256], P(None, 'depth', 'lat')
The draws below stay inside these ranges and needn't reach their ends.
Inputs may be any that keep to these rules, and one draw needn't show every extreme that they name: `frame_count`: some tile owns all 8 slots' frames in every draw.
All inputs are finite; a program needn't handle non-finite values. No bound on the sum of `frame_count` on one device may be relied on, other than what follows from the above.
Results may differ from the reference program's by a relative error of at most 0.0003.
Values may be sent and summed in bfloat16 or wider, within the bound.
No kernel may reach another device: no remote copies, remote signals or barrier semaphores. Data moves between devices by JAX's collectives and lax.ppermute only.
A program may use at most 64 MiB of HBM per device.

```python
import math
import jax
import jax.numpy as jnp
import numpy as np
from jax import lax

SX = 128
NY = 256
F_DEV = 8
NA = 32
REACH = 64
NZ = 64
NX = 8192
NF = 512
N_LAT = 64


def touch_ends(result, stream_key, smallest, top_value):
    spot = [jax.random.randint(jax.random.fold_in(stream_key, axis), (), 0, length) for axis, length in enumerate(result.shape)]
    longest = result.shape.index(max(result.shape))
    beside = spot[:longest] + [(spot[longest] + 1) % result.shape[longest]] + spot[longest + 1:]
    return result.at[tuple(spot)].set(smallest).at[tuple(beside)].set(top_value)


def steps_of(rng, dims, cuts, smallest, high):
    gain = 1.0
    for position, shards_of in cuts:
        draws = jax.random.uniform(jax.random.fold_in(jax.random.fold_in(rng, 6), position), (shards_of,), jnp.float32, smallest / len(cuts), high / len(cuts))
        gain = gain * jnp.repeat(jnp.exp(draws), dims[position] // shards_of).reshape((-1,) + (1,) * (len(dims) - 1 - position))
    return gain


def profile(amount, total, bound, lean):
    weights = [(1 << 20) // math.isqrt(standing ** lean) + 1 for standing in range(2, amount + 1)]
    surplus, holding = total - bound - (amount - 1), [1] * (amount - 1)
    while surplus > 0:
        candidates = [i for i in range(amount - 1) if holding[i] < bound]
        mass, remaining = sum([weights[i] for i in candidates]), surplus
        for i in candidates:
            more = min(bound - holding[i], max(1, remaining * weights[i] // mass), surplus)
            holding[i] = holding[i] + more
            surplus = surplus - more
    return np.array([bound] + holding)


def ragged(key, number_of, total, limit, slope):
    if number_of == 2:
        one = jax.random.randint(key, (), max(1, total - limit), min(limit, total - 1) + 1)
        return jnp.stack([one, total - one])
    sizes = jnp.asarray(profile(number_of, total, limit, slope), jnp.int32)
    twos = (number_of - 1) // 2
    donor, sink = sizes[1:1 + 2 * twos:2], sizes[2:2 + 2 * twos:2]
    slack = jnp.minimum(donor - 1, limit - sink)
    shifted = jax.random.randint(jax.random.fold_in(key, 1), (twos,), 0, 1 << 20) % (slack + 1)
    sizes = sizes.at[1:1 + 2 * twos:2].set(donor - shifted).at[2:2 + 2 * twos:2].set(sink + shifted)
    return sizes[jax.random.permutation(jax.random.fold_in(key, 2), number_of)]


def normal_values(key, extent, scale, most, pieces=(), kind=jnp.bfloat16):
    level = steps_of(key, extent, pieces, -0.22, 0.18) if pieces else 1.0
    entries = jax.random.normal(key, extent, jnp.float32) * scale * level
    return jnp.minimum(jnp.maximum(entries, -most), most).astype(kind)


def setup_inputs(seed: int = 0) -> dict:
    key_of = jax.random.split(jax.random.key(seed), 9)
    object_field = normal_values(key_of[0], (2, NZ, NX, NY), 1.0, 6.0, ((1, 8), (2, 64)))
    probe_field = normal_values(key_of[1], (2, SX, NY), 1.0, 6.0)
    intensity = jnp.clip(jnp.exp(math.log(4.0) - 3.6927934 * jax.random.uniform(key_of[2], (NF, SX, NY), jnp.float32) ** steps_of(key_of[2], (NF, SX, NY), ((0, 64),), -0.2, 0.2)), 0.099609375, 4.0).astype(jnp.bfloat16)
    depth_phase = jnp.clip(jax.random.uniform(key_of[3], (NA, NZ), jnp.float32, -3.140625, 3.140625), -3.140625, 3.140625)
    shear_rate = touch_ends(jax.random.randint(key_of[4], (NA,), 0 - REACH, REACH + 1), jax.random.fold_in(key_of[4], 1), 0 - REACH, REACH).astype(jnp.int32)
    positions = touch_ends(jax.random.randint(key_of[5], (NF,), 0 - REACH // 2, REACH // 2 + 1), jax.random.fold_in(key_of[5], 1), 0 - REACH // 2, (REACH // 2 + 1) - 1).astype(jnp.int32)
    angle_index = touch_ends(jax.random.randint(key_of[6], (NF,), 0, NA), jax.random.fold_in(key_of[6], 1), 0, NA - 1).astype(jnp.int32)
    frame_count = ragged(key_of[7], N_LAT, 5 * N_LAT * F_DEV // 8, F_DEV, 2).astype(jnp.int32)
    return dict(object_field=object_field, probe_field=probe_field, intensity=intensity, depth_phase=depth_phase, shear_rate=shear_rate, positions=positions, angle_index=angle_index, frame_count=frame_count)


def reference(object_field, probe_field, intensity, depth_phase, shear_rate, positions, angle_index, frame_count):
    padded = jnp.pad(object_field, ((0, 0), (0, 0), (REACH, REACH), (0, 0)))
    depth_cells = jnp.arange(NZ, dtype=jnp.int32)
    tile_rows = jnp.arange(SX, dtype=jnp.int32)
    cosine = jnp.cos(depth_phase.astype(jnp.float32))
    sine = jnp.sin(depth_phase.astype(jnp.float32))
    probe_real = probe_field[0].astype(jnp.float32)
    probe_imag = probe_field[1].astype(jnp.float32)
    scale = 1.0 / math.sqrt(NZ)

    def step_frame(frame, correction):
        frame = jnp.asarray(frame).astype(jnp.int32)
        owner = frame // F_DEV
        angle_row = angle_index[frame]
        shift = shear_rate[angle_row] * (2 * depth_cells - NZ) // (2 * NZ)
        starts = owner * SX + REACH + positions[frame] + shift
        rows = (starts[:, None] + tile_rows[None, :]).astype(jnp.int32)
        slices = padded[:, depth_cells[:, None], rows, :].astype(jnp.float32)
        ramp_real = cosine[angle_row][:, None, None]
        ramp_imag = sine[angle_row][:, None, None]
        sum_real = lax.optimization_barrier(jnp.sum(slices[0] * ramp_real - slices[1] * ramp_imag, axis=0)) * scale
        sum_imag = lax.optimization_barrier(jnp.sum(slices[0] * ramp_imag + slices[1] * ramp_real, axis=0)) * scale
        wave = probe_real * sum_real - probe_imag * sum_imag + 1j * (probe_real * sum_imag + probe_imag * sum_real)
        far_wave = jnp.fft.fft2(wave, norm='ortho')
        magnitude = jnp.abs(far_wave)
        amplitude = jnp.sqrt(intensity[frame].astype(jnp.float32))
        valid = (frame % F_DEV < frame_count[owner]).astype(jnp.float32)
        difference = far_wave * ((amplitude / jnp.maximum(magnitude, 0.5) - 1.0) * valid)
        update = jnp.fft.ifft2(difference, norm='ortho')
        update_real = jnp.real(update)
        update_imag = jnp.imag(update)
        back_real = probe_real * update_real + probe_imag * update_imag
        back_imag = probe_real * update_imag - probe_imag * update_real
        term_real = back_real[None] * ramp_real + back_imag[None] * ramp_imag
        term_imag = back_imag[None] * ramp_real - back_real[None] * ramp_imag
        return correction.at[:, depth_cells[:, None], rows, :].add(jnp.stack([term_real, term_imag]))
    correction = jnp.zeros((2, NZ, NX + 2 * REACH, NY), jnp.float32)
    correction = lax.fori_loop(0, NF, step_frame, correction)
    return correction[:, :, REACH:REACH + NX, :]
```

```python
import math

import jax
import jax.numpy as jnp
import ml_dtypes
import numpy as np
from jax import lax
from jax.experimental import pallas as pl
from jax.experimental.pallas import tpu as pltpu
from jax.sharding import PartitionSpec as P

INTERPRET = False
LANES = 128
HEAD = 16
STEPS = 128.0
TOP = 32700.0
SHIFTER = 12582912.0


def split_pair(table):
    high = table.astype(ml_dtypes.bfloat16)
    low = (table - high.astype(np.float64)).astype(ml_dtypes.bfloat16)
    return high, low


def dft_pair(length):
    index = np.arange(length, dtype=np.int64)
    theta = 2.0 * np.pi / length * (index[:, None] * index[None, :] % length)
    factor = 1.0 / math.sqrt(length)
    return np.cos(theta) * factor, np.sin(theta) * factor


def row_table(length):
    high, low = split_pair(np.concatenate(dft_pair(length), axis=0))
    return np.concatenate([high, low, high], axis=1)


def column_tables(length):
    return split_pair(np.concatenate(dft_pair(length), axis=1))


def column_code(peak):
    bounded = jnp.maximum(peak, 2.0**-100)
    return jnp.ceil(jnp.log(bounded) * (STEPS / math.log(2.0))) + 1.0


def code_gain(code):
    return TOP * jnp.exp(code * (-math.log(2.0) / STEPS))


def code_step(code):
    return jnp.exp(code * (math.log(2.0) / STEPS)) * (1.0 / TOP)


def coded(value, gain):
    rounded = (value * gain + SHIFTER) - SHIFTER
    return rounded.astype(jnp.int32).astype(jnp.int16)


def widened(value):
    return value.astype(jnp.int32).astype(jnp.float32)


def shift_of(shear, level, total):
    return lax.shift_right_arithmetic(shear * (2 * level - total), int(math.log2(2 * total)))


def exit_kernel(
    slab, positions, angles, shears, cosines, sines, own, low, high, out, extended, wave, *, total
):
    frame = pl.program_id(0)
    levels, tile = own.shape[1], own.shape[2]
    reach = tile // 2
    halves = own.shape[3] // LANES

    @pl.when(frame == 0)
    def _():
        def fill(level, carry):
            for part in range(2):
                rim = pl.ds((part * levels + level) * reach, reach)
                for half in range(halves):
                    lanes = slice(half * LANES, (half + 1) * LANES)
                    extended[part, level, half, :reach] = low[rim, lanes].astype(jnp.float32)
                    extended[part, level, half, reach : reach + tile] = own[
                        part, level, :, lanes
                    ].astype(jnp.float32)
                    extended[part, level, half, reach + tile :] = high[rim, lanes].astype(
                        jnp.float32
                    )
            return carry

        lax.fori_loop(0, levels, fill, 0)

    angle = angles[frame]
    shear = shears[angle]
    base = reach + positions[frame]
    first = slab[0] * levels
    starts = [base + shift_of(shear, first + level, total) for level in range(levels)]
    ramps = [(cosines[angle, level], sines[angle, level]) for level in range(levels)]
    for half in range(halves):
        lanes = slice(half * LANES, (half + 1) * LANES)
        peak = jnp.zeros((1, LANES), jnp.float32)
        for chunk in range(2):
            sum_real = jnp.zeros((reach, LANES), jnp.float32)
            sum_imag = jnp.zeros((reach, LANES), jnp.float32)
            for level in range(levels):
                rows = pl.ds(starts[level] + chunk * reach, reach)
                real = extended[0, level, half, rows]
                imag = extended[1, level, half, rows]
                ramp_real, ramp_imag = ramps[level]
                sum_real = sum_real + (real * ramp_real - imag * ramp_imag)
                sum_imag = sum_imag + (real * ramp_imag + imag * ramp_real)
            wave[0, chunk] = sum_real
            wave[1, chunk] = sum_imag
            top = jnp.maximum(jnp.abs(sum_real), jnp.abs(sum_imag))
            peak = jnp.maximum(peak, jnp.max(top, axis=0, keepdims=True))
        code = column_code(peak)
        gain = code_gain(code)
        for part in range(2):
            for chunk in range(2):
                at = (part * 2 + chunk) * reach
                out[0, at : at + reach, lanes] = coded(wave[part, chunk], gain)
        out[0, 4 * reach :, lanes] = (
            jnp.broadcast_to(code, (HEAD, LANES)).astype(jnp.int32).astype(jnp.int16)
        )


def halves_of(value):
    high = value.astype(jnp.bfloat16)
    low = (value - high.astype(jnp.float32)).astype(jnp.bfloat16)
    return high, low


def matmul(left, right):
    return jnp.dot(left, right, preferred_element_type=jnp.float32)


def row_products(table, real, imag):
    high, low = halves_of(jnp.concatenate([real, imag], axis=1))
    both = matmul(table[...], jnp.concatenate([high, high, low], axis=0))
    rows, columns = real.shape
    return (
        both[:rows, :columns],
        both[:rows, columns:],
        both[rows:, :columns],
        both[rows:, columns:],
    )


def column_products(table_high, table_low, real, imag):
    high, low = halves_of(jnp.concatenate([real, imag], axis=0))
    both = matmul(high, table_high[...])
    both = both + matmul(high, table_low[...])
    both = both + matmul(low, table_high[...])
    rows, columns = real.shape
    return (
        both[:rows, :columns],
        both[rows:, :columns],
        both[:rows, columns:],
        both[rows:, columns:],
    )


def frame_kernel(
    slot, count, partials, probe, intensity, row_ref, column_high, column_low, out, *, total
):
    frames = partials.shape[0]
    tile = probe.shape[1]
    reach = tile // 2
    sum_real = jnp.zeros(probe.shape[1:], jnp.float32)
    sum_imag = jnp.zeros(probe.shape[1:], jnp.float32)
    for source in range(frames):
        step = code_step(widened(partials[source, 4 * reach :])[:1])
        sum_real = sum_real + widened(partials[source, : 2 * reach]) * step
        sum_imag = sum_imag + widened(partials[source, 2 * reach : 4 * reach]) * step
    scale = 1.0 / math.sqrt(total)
    sum_real = sum_real * scale
    sum_imag = sum_imag * scale
    probe_real = probe[0].astype(jnp.float32)
    probe_imag = probe[1].astype(jnp.float32)
    wave_real = probe_real * sum_real - probe_imag * sum_imag
    wave_imag = probe_real * sum_imag + probe_imag * sum_real

    cos_real, cos_imag, sin_real, sin_imag = row_products(row_ref, wave_real, wave_imag)
    mid_real = cos_real + sin_imag
    mid_imag = cos_imag - sin_real
    cos_real, cos_imag, sin_real, sin_imag = column_products(
        column_high, column_low, mid_real, mid_imag
    )
    far_real = cos_real + sin_imag
    far_imag = cos_imag - sin_real

    magnitude = jnp.sqrt(far_real * far_real + far_imag * far_imag)
    amplitude = jnp.sqrt(intensity[0].astype(jnp.float32))
    valid = jnp.where(slot[0] < count[0], 1.0, 0.0).astype(jnp.float32)
    factor = (amplitude / jnp.maximum(magnitude, 0.5) - 1.0) * valid
    far_real = far_real * factor
    far_imag = far_imag * factor

    cos_real, cos_imag, sin_real, sin_imag = column_products(
        column_high, column_low, far_real, far_imag
    )
    mid_real = cos_real - sin_imag
    mid_imag = cos_imag + sin_real
    cos_real, cos_imag, sin_real, sin_imag = row_products(row_ref, mid_real, mid_imag)
    update_real = cos_real - sin_imag
    update_imag = cos_imag + sin_real

    back_real = probe_real * update_real + probe_imag * update_imag
    back_imag = probe_real * update_imag - probe_imag * update_real
    peak = jnp.max(
        jnp.maximum(jnp.abs(back_real), jnp.abs(back_imag)), axis=0, keepdims=True
    )
    code = column_code(peak)
    gain = code_gain(code)
    coded_real = coded(back_real, gain)
    coded_imag = coded(back_imag, gain)
    out[:reach] = coded_real[:reach]
    out[reach : 2 * reach] = coded_imag[:reach]
    out[2 * reach : 2 * reach + HEAD] = (
        jnp.broadcast_to(code, (HEAD, code.shape[1])).astype(jnp.int32).astype(jnp.int16)
    )
    out[2 * reach + HEAD : 3 * reach + HEAD] = coded_real[reach:]
    out[3 * reach + HEAD :] = coded_imag[reach:]


def own_kernel(
    slab, positions, angles, shears, cosines, sines, frames_ref, out, padded, *, total
):
    level = pl.program_id(0)
    levels = pl.num_programs(0)
    frames, tile = frames_ref.shape[0], out.shape[2]
    reach = tile // 2
    halves = out.shape[3] // LANES

    @pl.when(level == 0)
    def _():
        blank = jnp.zeros((reach, LANES), jnp.float32)

        def fill(frame, carry):
            for half in range(halves):
                lanes = slice(half * LANES, (half + 1) * LANES)
                head = frames_ref[frame, 2 * reach : 2 * reach + HEAD, lanes]
                step = code_step(widened(head)[:1])
                for part in range(2):
                    padded[part, frame, half, :reach] = blank
                    padded[part, frame, half, reach + tile :] = blank
                    at = part * reach
                    padded[part, frame, half, reach : 2 * reach] = (
                        widened(frames_ref[frame, at : at + reach, lanes]) * step
                    )
                    at = (2 + part) * reach + HEAD
                    padded[part, frame, half, 2 * reach : 3 * reach] = (
                        widened(frames_ref[frame, at : at + reach, lanes]) * step
                    )
            return carry

        lax.fori_loop(0, frames, fill, 0)

    here = slab[0] * levels + level
    starts, ramps = [], []
    for frame in range(frames):
        angle = angles[frame]
        starts.append(reach - positions[frame] - shift_of(shears[angle], here, total))
        ramps.append((cosines[angle, level], sines[angle, level]))
    for half in range(halves):
        lanes = slice(half * LANES, (half + 1) * LANES)
        for chunk in range(2):
            sum_real = jnp.zeros((reach, LANES), jnp.float32)
            sum_imag = jnp.zeros((reach, LANES), jnp.float32)
            for frame in range(frames):
                rows = pl.ds(starts[frame] + chunk * reach, reach)
                real = padded[0, frame, half, rows]
                imag = padded[1, frame, half, rows]
                ramp_real, ramp_imag = ramps[frame]
                sum_real = sum_real + (real * ramp_real + imag * ramp_imag)
                sum_imag = sum_imag + (imag * ramp_real - real * ramp_imag)
            rows = slice(chunk * reach, (chunk + 1) * reach)
            out[0, 0, rows, lanes] = sum_real
            out[1, 0, rows, lanes] = sum_imag


def rim_kernel(
    slab, below, above, shears, cosines, sines, lower, upper, inner, out, padded, *, total
):
    level = pl.program_id(0)
    levels = pl.num_programs(0)
    frames, tile = lower.shape[0], out.shape[2]
    reach = tile // 2
    halves = out.shape[3] // LANES

    @pl.when(level == 0)
    def _():
        blank = jnp.zeros((reach, LANES), jnp.float32)

        def fill(frame, carry):
            for half in range(halves):
                lanes = slice(half * LANES, (half + 1) * LANES)
                low_step = code_step(widened(lower[frame, :HEAD, lanes])[:1])
                high_step = code_step(widened(upper[frame, 2 * reach :, lanes])[:1])
                for part in range(2):
                    at = HEAD + part * reach
                    padded[0, part, frame, half, :reach] = (
                        widened(lower[frame, at : at + reach, lanes]) * low_step
                    )
                    padded[0, part, frame, half, reach:] = blank
                    at = part * reach
                    padded[1, part, frame, half, :reach] = blank
                    padded[1, part, frame, half, reach:] = (
                        widened(upper[frame, at : at + reach, lanes]) * high_step
                    )
            return carry

        lax.fori_loop(0, frames, fill, 0)

    here = slab[0] * levels + level
    for chunk, around in enumerate((below, above)):
        starts, ramps = [], []
        for frame in range(frames):
            angle = around[frames + frame]
            start = around[frame] + shift_of(shears[angle], here, total)
            if chunk == 0:
                starts.append(reach - jnp.maximum(start, 0))
            else:
                starts.append(-jnp.minimum(start, 0))
            ramps.append((cosines[angle, level], sines[angle, level]))
        for half in range(halves):
            lanes = slice(half * LANES, (half + 1) * LANES)
            at = slice(chunk * reach, (chunk + 1) * reach)
            sum_real = inner[0, 0, at, lanes]
            sum_imag = inner[1, 0, at, lanes]
            for frame in range(frames):
                rows = pl.ds(starts[frame], reach)
                real = padded[chunk, 0, frame, half, rows]
                imag = padded[chunk, 1, frame, half, rows]
                ramp_real, ramp_imag = ramps[frame]
                sum_real = sum_real + (real * ramp_real + imag * ramp_imag)
                sum_imag = sum_imag + (imag * ramp_real - real * ramp_imag)
            out[0, 0, at, lanes] = sum_real
            out[1, 0, at, lanes] = sum_imag


def scalars():
    return pl.BlockSpec(memory_space=pltpu.SMEM)


def resident(shape):
    return pl.BlockSpec(shape, lambda *_: (0,) * len(shape), pipeline_mode=pl.Buffered(1))


def params(mebibytes):
    return pltpu.CompilerParams(vmem_limit_bytes=mebibytes << 20)


def passed_along(value, steps):
    count = lax.axis_size("lat")
    initial, last = (max(0, -steps), min(count, count - steps))
    return lax.ppermute(value, "lat", [(source, source + steps) for source in range(initial, last)])


def shards(
    object_field,
    probe_field,
    intensity,
    depth_phase,
    shear_rate,
    positions,
    angle_index,
    frame_count,
):
    levels = object_field.shape[1]
    tile = object_field.shape[2]
    width = object_field.shape[3]
    frames = positions.shape[0]
    reach = tile // 2
    halves = width // LANES
    slabs = lax.axis_size("depth")
    total = levels * slabs
    slab = lax.axis_index("depth").astype(jnp.int32).reshape(1)
    coded_rows = 2 * tile + HEAD

    spots = jnp.concatenate([positions, angle_index]).astype(jnp.bfloat16)
    spots = jnp.pad(spots[None], ((0, HEAD - 1), (0, width - 2 * frames)))
    rim_rows = 2 * levels * reach
    last = jnp.concatenate([object_field[:, :, reach:].reshape(rim_rows, width), spots])
    start = jnp.concatenate([object_field[:, :, :reach].reshape(rim_rows, width), spots])
    low = passed_along(last, 1)
    high = passed_along(start, -1)
    below = low[rim_rows, : 2 * frames].astype(jnp.int32)
    above = high[rim_rows, : 2 * frames].astype(jnp.int32)
    cosines = jnp.cos(depth_phase)
    sines = jnp.sin(depth_phase)

    partials = pl.pallas_call(
        lambda *refs: exit_kernel(*refs, total=total),
        out_shape=jax.ShapeDtypeStruct((frames, coded_rows, width), jnp.int16),
        grid=(frames,),
        in_specs=[scalars()] * 6
        + [
            resident(object_field.shape),
            resident(low.shape),
            resident(high.shape),
        ],
        out_specs=pl.BlockSpec((1, coded_rows, width), lambda f: (f, 0, 0)),
        scratch_shapes=[
            pltpu.VMEM((2, levels, halves, 2 * tile, LANES), jnp.float32),
            pltpu.VMEM((2, 2, reach, LANES), jnp.float32),
        ],
        compiler_params=params(16),
        interpret=INTERPRET,
        name="exit_waves",
    )(slab, positions, angle_index, shear_rate, cosines, sines, object_field, low, high)

    received = lax.all_to_all(partials, "depth", 0, 0)

    table = jnp.asarray(row_table(tile))
    column_high, column_low = (jnp.asarray(t) for t in column_tables(width))
    back = pl.pallas_call(
        lambda *refs: frame_kernel(*refs, total=total),
        out_shape=jax.ShapeDtypeStruct((coded_rows, width), jnp.int16),
        grid_spec=pltpu.PrefetchScalarGridSpec(
            num_scalar_prefetch=2,
            grid=(1,),
            in_specs=[
                resident(received.shape),
                resident(probe_field.shape),
                pl.BlockSpec((1, tile, width), lambda i, slot, count: (slot[0], 0, 0)),
                resident(table.shape),
                resident(column_high.shape),
                resident(column_low.shape),
            ],
            out_specs=pl.BlockSpec((coded_rows, width), lambda *_: (0, 0)),
        ),
        compiler_params=params(16),
        interpret=INTERPRET,
        name="far_field",
    )(slab, frame_count, received, probe_field, intensity, table, column_high, column_low)

    gathered = lax.all_gather(back, "depth")
    lower = passed_along(gathered[:, tile:], 1)
    upper = passed_along(gathered[:, : tile + HEAD], -1)

    level_block = pl.BlockSpec((2, 1, tile, width), lambda z: (0, z, 0, 0))
    shape = jax.ShapeDtypeStruct((2, levels, tile, width), jnp.float32)
    inner = pl.pallas_call(
        lambda *refs: own_kernel(*refs, total=total),
        out_shape=shape,
        grid=(levels,),
        in_specs=[scalars()] * 6 + [resident(gathered.shape)],
        out_specs=level_block,
        scratch_shapes=[pltpu.VMEM((2, frames, halves, 2 * tile, LANES), jnp.float32)],
        compiler_params=params(16),
        cost_estimate=pl.CostEstimate(
            flops=frames * levels * tile * width * 8, bytes_accessed=4 << 20, transcendentals=0
        ),
        interpret=INTERPRET,
        name="own_frames",
    )(slab, positions, angle_index, shear_rate, cosines, sines, gathered)

    return pl.pallas_call(
        lambda *refs: rim_kernel(*refs, total=total),
        out_shape=shape,
        grid=(levels,),
        in_specs=[scalars()] * 6
        + [
            resident(lower.shape),
            resident(upper.shape),
            level_block,
        ],
        out_specs=level_block,
        scratch_shapes=[pltpu.VMEM((2, 2, frames, halves, tile, LANES), jnp.float32)],
        compiler_params=params(16),
        interpret=INTERPRET,
        name="neighbour_frames",
    )(slab, below, above, shear_rate, cosines, sines, lower, upper, inner)


def solution(mesh):
    placed = (
        P(None, "depth", "lat", None),
        P(),
        P("lat", None, None),
        P(None, "depth"),
        P(),
        P("lat"),
        P("lat"),
        P("lat"),
    )
    return jax.shard_map(
        shards, mesh=mesh, in_specs=placed, out_specs=P(None, "depth", "lat", None), check_vma=False
    )
```

```python
import math

import jax
import jax.numpy as jnp
import ml_dtypes
import numpy as np
from jax import lax
from jax.experimental import pallas as pl
from jax.experimental.pallas import tpu as pltpu
from jax.sharding import PartitionSpec as P

INTERPRET = False
PIECES = 1
LANES = 128
HEAD = 16
STEPS = 128.0
TOP = 32700.0
SHIFTER = 12582912.0


def split_pair(table):
    high = table.astype(ml_dtypes.bfloat16)
    low = (table - high.astype(np.float64)).astype(ml_dtypes.bfloat16)
    return high, low


def dft_pair(length):
    index = np.arange(length, dtype=np.int64)
    theta = 2.0 * np.pi / length * (index[:, None] * index[None, :] % length)
    factor = 1.0 / math.sqrt(length)
    return np.cos(theta) * factor, np.sin(theta) * factor


def row_table(length):
    high, low = split_pair(np.concatenate(dft_pair(length), axis=0))
    return np.concatenate([high, low, high], axis=1)


def column_tables(length):
    return split_pair(np.concatenate(dft_pair(length), axis=1))


def column_code(peak):
    bounded = jnp.maximum(peak, 2.0**-100)
    return jnp.ceil(jnp.log(bounded) * (STEPS / math.log(2.0))) + 1.0


def code_gain(code):
    return TOP * jnp.exp(code * (-math.log(2.0) / STEPS))


def code_step(code):
    return jnp.exp(code * (math.log(2.0) / STEPS)) * (1.0 / TOP)


def coded(value, gain):
    rounded = (value * gain + SHIFTER) - SHIFTER
    return rounded.astype(jnp.int32).astype(jnp.int16)


def widened(value):
    return value.astype(jnp.int32).astype(jnp.float32)


def shift_of(shear, level, total):
    return lax.shift_right_arithmetic(shear * (2 * level - total), int(math.log2(2 * total)))


def exit_kernel(
    slab, positions, angles, shears, cosines, sines, own, low, high, out, extended, wave, staged, sem
):
    frames = out.shape[0]
    levels, tile = own.shape[1], own.shape[2]
    reach = tile // 2
    halves = own.shape[3] // LANES
    total = 8 * levels
    first = slab[0] * levels

    def fill(level, carry):
        for part in range(2):
            rim = pl.ds((part * levels + level) * reach, reach)
            for half in range(halves):
                lanes = slice(half * LANES, (half + 1) * LANES)
                extended[part, level, half, :reach] = low[rim, lanes].astype(jnp.float32)
                extended[part, level, half, reach : reach + tile] = own[
                    part, level, :, lanes
                ].astype(jnp.float32)
                extended[part, level, half, reach + tile :] = high[rim, lanes].astype(jnp.float32)
        return carry

    lax.fori_loop(0, levels, fill, 0)

    def one(frame, carry):
        angle = angles[frame]
        shear = shears[angle]
        base = reach + positions[frame]
        starts = [base + shift_of(shear, first + level, total) for level in range(levels)]
        ramps = [
            (cosines[angle * levels + level], sines[angle * levels + level])
            for level in range(levels)
        ]
        for half in range(halves):
            lanes = slice(half * LANES, (half + 1) * LANES)
            peak = jnp.zeros((1, LANES), jnp.float32)
            for chunk in range(2):
                sum_real = jnp.zeros((reach, LANES), jnp.float32)
                sum_imag = jnp.zeros((reach, LANES), jnp.float32)
                for level in range(levels):
                    rows = pl.ds(starts[level] + chunk * reach, reach)
                    real = extended[0, level, half, rows]
                    imag = extended[1, level, half, rows]
                    ramp_real, ramp_imag = ramps[level]
                    sum_real = sum_real + (real * ramp_real - imag * ramp_imag)
                    sum_imag = sum_imag + (real * ramp_imag + imag * ramp_real)
                wave[0, chunk] = sum_real
                wave[1, chunk] = sum_imag
                top = jnp.maximum(jnp.abs(sum_real), jnp.abs(sum_imag))
                peak = jnp.maximum(peak, jnp.max(top, axis=0, keepdims=True))
            code = column_code(peak)
            gain = code_gain(code)
            for part in range(2):
                for chunk in range(2):
                    at = (part * 2 + chunk) * reach
                    staged[frame, at : at + reach, lanes] = coded(wave[part, chunk], gain)
            staged[frame, 4 * reach :, lanes] = (
                jnp.broadcast_to(code, (HEAD, LANES)).astype(jnp.int32).astype(jnp.int16)
            )
        pltpu.make_async_copy(staged.at[frame], out.at[frame], sem).start()
        return carry

    lax.fori_loop(0, frames, one, 0)
    pltpu.make_async_copy(staged, out, sem).wait()


def halves_of(value):
    high = value.astype(jnp.bfloat16)
    low = (value - high.astype(jnp.float32)).astype(jnp.bfloat16)
    return high, low


def matmul(left, right):
    return jnp.dot(left, right, preferred_element_type=jnp.float32)


def row_products(table, real, imag):
    high, low = halves_of(jnp.concatenate([real, imag], axis=1))
    both = matmul(table[...], jnp.concatenate([high, high, low], axis=0))
    rows, columns = real.shape
    return (
        both[:rows, :columns],
        both[:rows, columns:],
        both[rows:, :columns],
        both[rows:, columns:],
    )


def column_products(table_high, table_low, real, imag):
    high, low = halves_of(jnp.concatenate([real, imag], axis=0))
    both = matmul(high, table_high[...])
    both = both + matmul(high, table_low[...])
    both = both + matmul(low, table_high[...])
    rows, columns = real.shape
    return (
        both[:rows, :columns],
        both[rows:, :columns],
        both[:rows, columns:],
        both[rows:, columns:],
    )


def frame_kernel(
    slot,
    count,
    *refs,
    total,
):
    *parts, probe, intensity, row_ref, column_high, column_low, out, high_out, low_out = refs
    tile = probe.shape[1]
    reach = tile // 2
    sums_real, sums_imag = [], []
    for partials in parts:
        sum_real = jnp.zeros((tile, partials.shape[2]), jnp.float32)
        sum_imag = jnp.zeros((tile, partials.shape[2]), jnp.float32)
        for source in range(partials.shape[0]):
            step = code_step(widened(partials[source, 4 * reach :])[:1])
            sum_real = sum_real + widened(partials[source, : 2 * reach]) * step
            sum_imag = sum_imag + widened(partials[source, 2 * reach : 4 * reach]) * step
        sums_real.append(sum_real)
        sums_imag.append(sum_imag)
    sum_real = jnp.concatenate(sums_real, axis=1)
    sum_imag = jnp.concatenate(sums_imag, axis=1)
    scale = 1.0 / math.sqrt(total)
    sum_real = sum_real * scale
    sum_imag = sum_imag * scale
    probe_real = probe[0].astype(jnp.float32)
    probe_imag = probe[1].astype(jnp.float32)
    wave_real = probe_real * sum_real - probe_imag * sum_imag
    wave_imag = probe_real * sum_imag + probe_imag * sum_real

    cos_real, cos_imag, sin_real, sin_imag = row_products(row_ref, wave_real, wave_imag)
    mid_real = cos_real + sin_imag
    mid_imag = cos_imag - sin_real
    cos_real, cos_imag, sin_real, sin_imag = column_products(
        column_high, column_low, mid_real, mid_imag
    )
    far_real = cos_real + sin_imag
    far_imag = cos_imag - sin_real

    magnitude = jnp.sqrt(far_real * far_real + far_imag * far_imag)
    amplitude = jnp.sqrt(intensity[0].astype(jnp.float32))
    valid = jnp.where(slot[0] < count[0], 1.0, 0.0).astype(jnp.float32)
    factor = (amplitude / jnp.maximum(magnitude, 0.5) - 1.0) * valid
    far_real = far_real * factor
    far_imag = far_imag * factor

    cos_real, cos_imag, sin_real, sin_imag = column_products(
        column_high, column_low, far_real, far_imag
    )
    mid_real = cos_real - sin_imag
    mid_imag = cos_imag + sin_real
    cos_real, cos_imag, sin_real, sin_imag = row_products(row_ref, mid_real, mid_imag)
    update_real = cos_real - sin_imag
    update_imag = cos_imag + sin_real

    back_real = probe_real * update_real + probe_imag * update_imag
    back_imag = probe_real * update_imag - probe_imag * update_real
    peak = jnp.max(
        jnp.maximum(jnp.abs(back_real), jnp.abs(back_imag)), axis=0, keepdims=True
    )
    code = column_code(peak)
    gain = code_gain(code)
    coded_real = coded(back_real, gain)
    coded_imag = coded(back_imag, gain)
    head = jnp.broadcast_to(code, (HEAD, code.shape[1])).astype(jnp.int32).astype(jnp.int16)
    out[: 2 * reach] = coded_real
    out[2 * reach : 4 * reach] = coded_imag
    out[4 * reach :] = head
    low_out[:reach] = coded_real[:reach]
    low_out[reach : 2 * reach] = coded_imag[:reach]
    low_out[2 * reach :] = head
    high_out[:reach] = coded_real[reach:]
    high_out[reach : 2 * reach] = coded_imag[reach:]
    high_out[2 * reach :] = head


def correction_kernel(
    slab, positions, angles, below, above, shears, cosines, sines, *refs
):
    mine, theirs, out, inner, rims, staged, sem = refs
    levels, tile = out.shape[1], out.shape[2]
    reach = tile // 2
    halves = out.shape[3] // LANES
    share = mine.shape[0]
    frames = 2 * share
    total = 8 * levels
    blank = jnp.zeros((reach, LANES), jnp.float32)
    bottom, top = 4 * reach + HEAD, 6 * reach + 2 * HEAD

    for source, odd in ((mine, slab[0] & 1), (theirs, 1 - (slab[0] & 1))):

        def fill(item, carry, source=source, odd=odd):
            frame = 2 * item + odd
            for half in range(halves):
                lanes = slice(half * LANES, (half + 1) * LANES)

                def step_at(row):
                    return code_step(widened(source[item, row : row + HEAD, lanes])[:1])

                step = step_at(4 * reach)
                low_step = step_at(bottom + 2 * reach)
                high_step = step_at(top + 2 * reach)
                for part in range(2):
                    inner[part, frame, half, :reach] = blank
                    at = 2 * part * reach
                    inner[part, frame, half, reach : reach + tile] = (
                        widened(source[item, at : at + tile, lanes]) * step
                    )
                    inner[part, frame, half, reach + tile :] = blank
                    at = bottom + part * reach
                    rims[0, part, frame, half, :reach] = (
                        widened(source[item, at : at + reach, lanes]) * low_step
                    )
                    rims[0, part, frame, half, reach:] = blank
                    at = top + part * reach
                    rims[1, part, frame, half, :reach] = blank
                    rims[1, part, frame, half, reach:] = (
                        widened(source[item, at : at + reach, lanes]) * high_step
                    )
            return carry

        lax.fori_loop(0, share, fill, 0)

    def one(level, carry):
        here = slab[0] * levels + level
        starts, ramps = [], []
        for frame in range(frames):
            angle = angles[frame]
            starts.append(reach - positions[frame] - shift_of(shears[angle], here, total))
            ramps.append((cosines[angle * levels + level], sines[angle * levels + level]))
        for chunk, around in enumerate((below, above)):
            rim_starts, rim_ramps = [], []
            for frame in range(frames):
                angle = around[frames + frame]
                start = around[frame] + shift_of(shears[angle], here, total)
                if chunk == 0:
                    rim_starts.append(reach - jnp.maximum(start, 0))
                else:
                    rim_starts.append(-jnp.minimum(start, 0))
                rim_ramps.append((cosines[angle * levels + level], sines[angle * levels + level]))
            at = slice(chunk * reach, (chunk + 1) * reach)
            for half in range(halves):
                lanes = slice(half * LANES, (half + 1) * LANES)
                sum_real = jnp.zeros((reach, LANES), jnp.float32)
                sum_imag = jnp.zeros((reach, LANES), jnp.float32)
                for frame in range(frames):
                    rows = pl.ds(starts[frame] + chunk * reach, reach)
                    rim_rows = pl.ds(rim_starts[frame], reach)
                    for real, imag, (ramp_real, ramp_imag) in (
                        (inner[0, frame, half, rows], inner[1, frame, half, rows], ramps[frame]),
                        (
                            rims[chunk, 0, frame, half, rim_rows],
                            rims[chunk, 1, frame, half, rim_rows],
                            rim_ramps[frame],
                        ),
                    ):
                        sum_real = sum_real + (real * ramp_real + imag * ramp_imag)
                        sum_imag = sum_imag + (imag * ramp_real - real * ramp_imag)
                staged[0, level, at, lanes] = sum_real
                staged[1, level, at, lanes] = sum_imag
        for part in range(2):
            pltpu.make_async_copy(staged.at[part, level], out.at[part, level], sem).start()
        return carry

    lax.fori_loop(0, levels, one, 0)
    pltpu.make_async_copy(staged, out, sem).wait()


def scalars():
    return pl.BlockSpec(memory_space=pltpu.SMEM)


def resident(shape):
    return pl.BlockSpec(shape, lambda *_: (0,) * len(shape), pipeline_mode=pl.Buffered(1))


def params(mebibytes):
    return pltpu.CompilerParams(vmem_limit_bytes=mebibytes << 20)


def passed_along(value, steps):
    count = lax.axis_size("lat")
    initial, last = (max(0, -steps), min(count, count - steps))
    return lax.ppermute(value, "lat", [(source, source + steps) for source in range(initial, last)])


def shards(
    object_field,
    probe_field,
    intensity,
    depth_phase,
    shear_rate,
    positions,
    angle_index,
    frame_count,
):
    levels = object_field.shape[1]
    tile = object_field.shape[2]
    width = object_field.shape[3]
    frames = positions.shape[0]
    reach = tile // 2
    halves = width // LANES
    slabs = lax.axis_size("depth")
    total = levels * slabs
    slab = lax.axis_index("depth").astype(jnp.int32).reshape(1)
    coded_rows = 2 * tile + HEAD

    spots = jnp.concatenate([positions, angle_index]).astype(jnp.bfloat16)
    spots = jnp.pad(spots[None], ((0, HEAD - 1), (0, width - 2 * frames)))
    rim_rows = 2 * levels * reach
    last = object_field[:, :, reach:].reshape(rim_rows, width)
    start = object_field[:, :, :reach].reshape(rim_rows, width)
    span = width // PIECES
    rims = []
    for piece in range(PIECES):
        lanes = slice(piece * span, (piece + 1) * span)
        pair = [last[:, lanes], start[:, lanes]]
        if piece == 0:
            pair = [jnp.concatenate([rows, spots[:, lanes]]) for rows in pair]
        rims.append((passed_along(pair[0], 1), passed_along(pair[1], -1)))
    below = rims[0][0][rim_rows, : 2 * frames].astype(jnp.int32)
    above = rims[0][1][rim_rows, : 2 * frames].astype(jnp.int32)
    cosines = jnp.cos(depth_phase).reshape(-1)
    sines = jnp.sin(depth_phase).reshape(-1)

    received = []
    for piece, (low, high) in enumerate(rims):
        block = (2, levels, tile, span)
        partials = pl.pallas_call(
            exit_kernel,
            out_shape=jax.ShapeDtypeStruct((frames, coded_rows, span), jnp.int16),
            grid=(1,),
            in_specs=[scalars()] * 6
            + [
                pl.BlockSpec(
                    block, lambda _, p=piece: (0, 0, 0, p), pipeline_mode=pl.Buffered(1)
                ),
                resident(low.shape),
                resident(high.shape),
            ],
            out_specs=pl.BlockSpec(memory_space=pl.ANY),
            scratch_shapes=[
                pltpu.VMEM((2, levels, span // LANES, 2 * tile, LANES), jnp.float32),
                pltpu.VMEM((2, 2, reach, LANES), jnp.float32),
                pltpu.VMEM((frames, coded_rows, span), jnp.int16),
                pltpu.SemaphoreType.DMA(()),
            ],
            compiler_params=params(16),
            interpret=INTERPRET,
            name=f"exit_waves_{piece}",
        )(slab, positions, angle_index, shear_rate, cosines, sines, object_field, low, high)
        received.append(lax.all_to_all(partials, "depth", 0, 0))

    table = jnp.asarray(row_table(tile))
    column_high, column_low = (jnp.asarray(t) for t in column_tables(width))
    half_rows = tile + HEAD
    back, to_above, to_below = pl.pallas_call(
        lambda *refs: frame_kernel(*refs, total=total),
        out_shape=[
            jax.ShapeDtypeStruct((rows, width), jnp.int16)
            for rows in (coded_rows, half_rows, half_rows)
        ],
        grid_spec=pltpu.PrefetchScalarGridSpec(
            num_scalar_prefetch=2,
            grid=(1,),
            in_specs=[resident(part.shape) for part in received]
            + [
                resident(probe_field.shape),
                pl.BlockSpec((1, tile, width), lambda i, slot, count: (slot[0], 0, 0)),
                resident(table.shape),
                resident(column_high.shape),
                resident(column_low.shape),
            ],
            out_specs=[
                pl.BlockSpec((rows, width), lambda *_: (0, 0))
                for rows in (coded_rows, half_rows, half_rows)
            ],
        ),
        compiler_params=params(16),
        interpret=INTERPRET,
        name="far_field",
    )(slab, frame_count, *received, probe_field, intensity, table, column_high, column_low)

    bundle = jnp.concatenate([back, passed_along(to_above, 1), passed_along(to_below, -1)])
    lanes_of = [[d for d in range(slabs) if d % 2 == core] for core in range(2)]
    mine = lax.all_gather(bundle, "depth", axis_index_groups=lanes_of)
    theirs = lax.ppermute(mine, "depth", [(d, d ^ 1) for d in range(slabs)])

    return pl.pallas_call(
        correction_kernel,
        out_shape=jax.ShapeDtypeStruct((2, levels, tile, width), jnp.float32),
        grid=(1,),
        in_specs=[scalars()] * 8 + [resident(mine.shape), resident(theirs.shape)],
        out_specs=pl.BlockSpec(memory_space=pl.ANY),
        scratch_shapes=[
            pltpu.VMEM((2, frames, halves, 2 * tile, LANES), jnp.float32),
            pltpu.VMEM((2, 2, frames, halves, tile, LANES), jnp.float32),
            pltpu.VMEM((2, levels, tile, width), jnp.float32),
            pltpu.SemaphoreType.DMA(()),
        ],
        compiler_params=params(24),
        interpret=INTERPRET,
        name="corrections",
    )(slab, positions, angle_index, below, above, shear_rate, cosines, sines, mine, theirs)


def solution(mesh):
    placed = (
        P(None, "depth", "lat", None),
        P(),
        P("lat", None, None),
        P(None, "depth"),
        P(),
        P("lat"),
        P("lat"),
        P("lat"),
    )
    return jax.shard_map(
        shards, mesh=mesh, in_specs=placed, out_specs=P(None, "depth", "lat", None), check_vma=False
    )
```

```python
import math

import jax
import jax.numpy as jnp
import ml_dtypes
import numpy as np
from jax import lax
from jax.experimental import pallas as pl
from jax.experimental.pallas import tpu as pltpu
from jax.sharding import PartitionSpec as P

INTERPRET = False
LANES = 128
HEAD = 16
STEPS = 128.0
TOP = 32700.0
SHIFTER = 12582912.0


def split_pair(table):
    high = table.astype(ml_dtypes.bfloat16)
    low = (table - high.astype(np.float64)).astype(ml_dtypes.bfloat16)
    return high, low


def dft_pair(length):
    index = np.arange(length, dtype=np.int64)
    theta = 2.0 * np.pi / length * (index[:, None] * index[None, :] % length)
    factor = 1.0 / math.sqrt(length)
    return np.cos(theta) * factor, np.sin(theta) * factor


def row_table(length):
    high, low = split_pair(np.concatenate(dft_pair(length), axis=0))
    return np.concatenate([high, low, high], axis=1)


def column_tables(length):
    return split_pair(np.concatenate(dft_pair(length), axis=1))


def column_code(peak):
    bounded = jnp.maximum(peak, 2.0**-100)
    return jnp.ceil(jnp.log(bounded) * (STEPS / math.log(2.0))) + 1.0


def code_gain(code):
    return TOP * jnp.exp(code * (-math.log(2.0) / STEPS))


def code_step(code):
    return jnp.exp(code * (math.log(2.0) / STEPS)) * (1.0 / TOP)


def coded(value, gain):
    rounded = (value * gain + SHIFTER) - SHIFTER
    return rounded.astype(jnp.int32).astype(jnp.int16)


def widened(value):
    return value.astype(jnp.int32).astype(jnp.float32)


def shift_of(shear, level, total):
    return lax.shift_right_arithmetic(shear * (2 * level - total), int(math.log2(2 * total)))


def exit_kernel(
    place, positions, angles, shears, cosines, sines, own, near, far, out, extended, wave, staged, sem
):
    frames = out.shape[0]
    levels, tile = own.shape[1], own.shape[2]
    reach = tile // 2
    halves = own.shape[3] // LANES
    total = 8 * levels
    first = place[0] * levels
    near_at = pl.multiple_of((1 - place[1]) * (reach + tile), reach)
    far_at = pl.multiple_of(place[1] * (reach + tile), reach)

    def fill(level, carry):
        for part in range(2):
            rim = pl.ds(pl.multiple_of((part * levels + level) * reach, reach), reach)
            for half in range(halves):
                lanes = slice(half * LANES, (half + 1) * LANES)
                extended[part, level, half, pl.ds(near_at, reach)] = near[rim, lanes].astype(
                    jnp.float32
                )
                extended[part, level, half, reach : reach + tile] = own[
                    part, level, :, lanes
                ].astype(jnp.float32)
                extended[part, level, half, pl.ds(far_at, reach)] = far[rim, lanes].astype(
                    jnp.float32
                )
        return carry

    lax.fori_loop(0, levels, fill, 0)

    def one(frame, carry):
        angle = angles[frame]
        shear = shears[angle]
        base = reach + positions[frame]
        starts = [base + shift_of(shear, first + level, total) for level in range(levels)]
        ramps = [
            (cosines[angle * levels + level], sines[angle * levels + level])
            for level in range(levels)
        ]
        for half in range(halves):
            lanes = slice(half * LANES, (half + 1) * LANES)
            peak = jnp.zeros((1, LANES), jnp.float32)
            for chunk in range(2):
                sum_real = jnp.zeros((reach, LANES), jnp.float32)
                sum_imag = jnp.zeros((reach, LANES), jnp.float32)
                for level in range(levels):
                    rows = pl.ds(starts[level] + chunk * reach, reach)
                    real = extended[0, level, half, rows]
                    imag = extended[1, level, half, rows]
                    ramp_real, ramp_imag = ramps[level]
                    sum_real = sum_real + (real * ramp_real - imag * ramp_imag)
                    sum_imag = sum_imag + (real * ramp_imag + imag * ramp_real)
                wave[0, chunk] = sum_real
                wave[1, chunk] = sum_imag
                top = jnp.maximum(jnp.abs(sum_real), jnp.abs(sum_imag))
                peak = jnp.maximum(peak, jnp.max(top, axis=0, keepdims=True))
            code = column_code(peak)
            gain = code_gain(code)
            for part in range(2):
                for chunk in range(2):
                    at = (part * 2 + chunk) * reach
                    staged[frame, at : at + reach, lanes] = coded(wave[part, chunk], gain)
            staged[frame, 4 * reach :, lanes] = (
                jnp.broadcast_to(code, (HEAD, LANES)).astype(jnp.int32).astype(jnp.int16)
            )
        pltpu.make_async_copy(staged.at[frame], out.at[frame], sem).start()
        return carry

    lax.fori_loop(0, frames, one, 0)
    pltpu.make_async_copy(staged, out, sem).wait()


def halves_of(value):
    high = value.astype(jnp.bfloat16)
    low = (value - high.astype(jnp.float32)).astype(jnp.bfloat16)
    return high, low


def matmul(left, right):
    return jnp.dot(left, right, preferred_element_type=jnp.float32)


def row_products(table, real, imag):
    high, low = halves_of(jnp.concatenate([real, imag], axis=1))
    both = matmul(table[...], jnp.concatenate([high, high, low], axis=0))
    rows, columns = real.shape
    return (
        both[:rows, :columns],
        both[:rows, columns:],
        both[rows:, :columns],
        both[rows:, columns:],
    )


def column_products(table_high, table_low, real, imag):
    high, low = halves_of(jnp.concatenate([real, imag], axis=0))
    both = matmul(high, table_high[...])
    both = both + matmul(high, table_low[...])
    both = both + matmul(low, table_high[...])
    rows, columns = real.shape
    return (
        both[:rows, :columns],
        both[rows:, :columns],
        both[:rows, columns:],
        both[rows:, columns:],
    )


def frame_kernel(
    place,
    count,
    *refs,
    total,
):
    *parts, probe, intensity, row_ref, column_high, column_low, out, near_out, far_out = refs
    tile = probe.shape[1]
    reach = tile // 2
    sums_real, sums_imag = [], []
    for partials in parts:
        sum_real = jnp.zeros((tile, partials.shape[2]), jnp.float32)
        sum_imag = jnp.zeros((tile, partials.shape[2]), jnp.float32)
        for source in range(partials.shape[0]):
            step = code_step(widened(partials[source, 4 * reach :])[:1])
            sum_real = sum_real + widened(partials[source, : 2 * reach]) * step
            sum_imag = sum_imag + widened(partials[source, 2 * reach : 4 * reach]) * step
        sums_real.append(sum_real)
        sums_imag.append(sum_imag)
    sum_real = jnp.concatenate(sums_real, axis=1)
    sum_imag = jnp.concatenate(sums_imag, axis=1)
    scale = 1.0 / math.sqrt(total)
    sum_real = sum_real * scale
    sum_imag = sum_imag * scale
    probe_real = probe[0].astype(jnp.float32)
    probe_imag = probe[1].astype(jnp.float32)
    wave_real = probe_real * sum_real - probe_imag * sum_imag
    wave_imag = probe_real * sum_imag + probe_imag * sum_real

    cos_real, cos_imag, sin_real, sin_imag = row_products(row_ref, wave_real, wave_imag)
    mid_real = cos_real + sin_imag
    mid_imag = cos_imag - sin_real
    cos_real, cos_imag, sin_real, sin_imag = column_products(
        column_high, column_low, mid_real, mid_imag
    )
    far_real = cos_real + sin_imag
    far_imag = cos_imag - sin_real

    magnitude = jnp.sqrt(far_real * far_real + far_imag * far_imag)
    amplitude = jnp.sqrt(intensity[place[0]].astype(jnp.float32))
    valid = jnp.where(place[0] < count[0], 1.0, 0.0).astype(jnp.float32)
    factor = (amplitude / jnp.maximum(magnitude, 0.5) - 1.0) * valid
    far_real = far_real * factor
    far_imag = far_imag * factor

    cos_real, cos_imag, sin_real, sin_imag = column_products(
        column_high, column_low, far_real, far_imag
    )
    mid_real = cos_real - sin_imag
    mid_imag = cos_imag + sin_real
    cos_real, cos_imag, sin_real, sin_imag = row_products(row_ref, mid_real, mid_imag)
    update_real = cos_real - sin_imag
    update_imag = cos_imag + sin_real

    back_real = probe_real * update_real + probe_imag * update_imag
    back_imag = probe_real * update_imag - probe_imag * update_real
    peak = jnp.max(
        jnp.maximum(jnp.abs(back_real), jnp.abs(back_imag)), axis=0, keepdims=True
    )
    code = column_code(peak)
    gain = code_gain(code)
    coded_real = coded(back_real, gain)
    coded_imag = coded(back_imag, gain)
    head = jnp.broadcast_to(code, (HEAD, code.shape[1])).astype(jnp.int32).astype(jnp.int16)
    out[: 2 * reach] = coded_real
    out[2 * reach : 4 * reach] = coded_imag
    out[4 * reach :] = head

    def rims(first_out, last_out):
        first_out[:reach] = coded_real[:reach]
        first_out[reach : 2 * reach] = coded_imag[:reach]
        first_out[2 * reach :] = head
        last_out[:reach] = coded_real[reach:]
        last_out[reach : 2 * reach] = coded_imag[reach:]
        last_out[2 * reach :] = head

    @pl.when(place[1] == 0)
    def _():
        rims(far_out, near_out)

    @pl.when(place[1] == 1)
    def _():
        rims(near_out, far_out)


def correction_kernel(place, positions, angles, below, above, shears, cosines, sines, *refs):
    gathered, out, inner, rims, staged, sem = refs
    levels, tile = out.shape[1], out.shape[2]
    reach = tile // 2
    halves = out.shape[3] // LANES
    frames = gathered.shape[0]
    total = 8 * levels
    blank = jnp.zeros((reach, LANES), jnp.float32)
    head_at = 4 * reach
    near_at = head_at + HEAD
    far_at = near_at + 2 * reach + HEAD
    lower_at = pl.multiple_of(jnp.where(place[1] == 0, far_at, near_at), HEAD)
    upper_at = pl.multiple_of(jnp.where(place[1] == 0, near_at, far_at), HEAD)
    for part in range(2):
        for half in range(halves):
            inner[part, half, :reach] = blank

    def fill(frame, carry):
        own = pl.multiple_of(reach + frame * 3 * reach, reach)
        rim = pl.multiple_of(frame * 3 * reach, reach)
        for half in range(halves):
            lanes = slice(half * LANES, (half + 1) * LANES)

            def step_at(row):
                return code_step(widened(gathered[frame, pl.ds(row, HEAD), lanes])[:1])

            step = step_at(head_at)
            lower_step = step_at(lower_at + 2 * reach)
            upper_step = step_at(upper_at + 2 * reach)
            for part in range(2):
                at = 2 * part * reach
                inner[part, half, pl.ds(own, tile)] = (
                    widened(gathered[frame, at : at + tile, lanes]) * step
                )
                inner[part, half, pl.ds(own + tile, reach)] = blank
                at = lower_at + part * reach
                rims[part, half, pl.ds(rim, reach)] = (
                    widened(gathered[frame, pl.ds(at, reach), lanes]) * lower_step
                )
                rims[part, half, pl.ds(rim + reach, reach)] = blank
                at = upper_at + part * reach
                rims[part, half, pl.ds(rim + 2 * reach, reach)] = (
                    widened(gathered[frame, pl.ds(at, reach), lanes]) * upper_step
                )
        return carry

    lax.fori_loop(0, frames, fill, 0, unroll=True)

    def one(level, carry):
        here = place[0] * levels + level
        starts, ramps = [], []
        for frame in range(frames):
            angle = angles[frame]
            start = positions[frame] + shift_of(shears[angle], here, total)
            starts.append((3 * frame + 1) * reach - start)
            ramps.append((cosines[angle * levels + level], sines[angle * levels + level]))
        for chunk, around in enumerate((below, above)):
            rim_starts, rim_ramps = [], []
            for frame in range(frames):
                angle = around[frames + frame]
                start = around[frame] + shift_of(shears[angle], here, total)
                if chunk == 0:
                    rim_starts.append((3 * frame + 1) * reach - jnp.maximum(start, 0))
                else:
                    rim_starts.append((3 * frame + 1) * reach - jnp.minimum(start, 0))
                rim_ramps.append((cosines[angle * levels + level], sines[angle * levels + level]))
            at = slice(chunk * reach, (chunk + 1) * reach)
            for half in range(halves):
                lanes = slice(half * LANES, (half + 1) * LANES)
                sum_real = jnp.zeros((reach, LANES), jnp.float32)
                sum_imag = jnp.zeros((reach, LANES), jnp.float32)
                for frame in range(frames):
                    for source, first, (ramp_real, ramp_imag) in (
                        (inner, starts[frame] + chunk * reach, ramps[frame]),
                        (rims, rim_starts[frame], rim_ramps[frame]),
                    ):
                        real = source[0, half, pl.ds(first, reach)]
                        imag = source[1, half, pl.ds(first, reach)]
                        sum_real = sum_real + (real * ramp_real + imag * ramp_imag)
                        sum_imag = sum_imag + (imag * ramp_real - real * ramp_imag)
                staged[0, level, at, lanes] = sum_real
                staged[1, level, at, lanes] = sum_imag
        for part in range(2):
            pltpu.make_async_copy(staged.at[part, level], out.at[part, level], sem).start()
        return carry

    lax.fori_loop(0, levels, one, 0)
    pltpu.make_async_copy(staged, out, sem).wait()


def scalars():
    return pl.BlockSpec(memory_space=pltpu.SMEM)


def resident():
    return pl.BlockSpec(memory_space=pltpu.VMEM)


def params(mebibytes):
    return pltpu.CompilerParams(vmem_limit_bytes=mebibytes << 20)


def exchanged(value, shift):
    count = lax.axis_size("lat")
    pairs = [(i, ((i + shift) ^ 1) - shift) for i in range(count)]
    return lax.ppermute(value, "lat", [(i, j) for i, j in pairs if 0 <= j < count])


def shards(
    object_field,
    probe_field,
    intensity,
    depth_phase,
    shear_rate,
    positions,
    angle_index,
    frame_count,
):
    levels = object_field.shape[1]
    tile = object_field.shape[2]
    width = object_field.shape[3]
    frames = positions.shape[0]
    reach = tile // 2
    halves = width // LANES
    slabs = lax.axis_size("depth")
    total = levels * slabs
    odd = lax.axis_index("lat").astype(jnp.int32) & 1
    place = jnp.stack([lax.axis_index("depth").astype(jnp.int32), odd])
    coded_rows = 2 * tile + HEAD

    spots = jnp.concatenate([positions, angle_index]).astype(jnp.bfloat16)
    spots = jnp.pad(spots[None], ((0, HEAD - 1), (0, width - 2 * frames)))
    rim_rows = 2 * levels * reach
    last = object_field[:, :, reach:].reshape(rim_rows, width)
    first = object_field[:, :, :reach].reshape(rim_rows, width)
    near = jnp.concatenate([jnp.where(odd == 0, last, first), spots])
    far = jnp.concatenate([jnp.where(odd == 0, first, last), spots])
    near = exchanged(near, 0)
    far = exchanged(far, 1)
    near_spots = near[rim_rows, : 2 * frames].astype(jnp.int32)
    far_spots = far[rim_rows, : 2 * frames].astype(jnp.int32)
    below = jnp.where(odd == 0, far_spots, near_spots)
    above = jnp.where(odd == 0, near_spots, far_spots)
    cosines = jnp.cos(depth_phase).reshape(-1)
    sines = jnp.sin(depth_phase).reshape(-1)

    partials = pl.pallas_call(
        exit_kernel,
        out_shape=jax.ShapeDtypeStruct((frames, coded_rows, width), jnp.int16),
        in_specs=[scalars()] * 6 + [resident()] * 3,
        out_specs=pl.BlockSpec(memory_space=pl.ANY),
        scratch_shapes=[
            pltpu.VMEM((2, levels, halves, 2 * tile, LANES), jnp.float32),
            pltpu.VMEM((2, 2, reach, LANES), jnp.float32),
            pltpu.VMEM((frames, coded_rows, width), jnp.int16),
            pltpu.SemaphoreType.DMA(()),
        ],
        compiler_params=params(16),
        interpret=INTERPRET,
        name="exit_waves",
    )(place, positions, angle_index, shear_rate, cosines, sines, object_field, near, far)
    received = lax.all_to_all(partials, "depth", 0, 0)

    table = jnp.asarray(row_table(tile))
    column_high, column_low = (jnp.asarray(t) for t in column_tables(width))
    half_rows = tile + HEAD
    back, near, far = pl.pallas_call(
        lambda *refs: frame_kernel(*refs, total=total),
        out_shape=[
            jax.ShapeDtypeStruct((rows, width), jnp.int16)
            for rows in (coded_rows, half_rows, half_rows)
        ],
        in_specs=[scalars()] * 2 + [resident()] * 6,
        out_specs=[resident()] * 3,
        compiler_params=params(16),
        interpret=INTERPRET,
        name="far_field",
    )(place, frame_count, received, probe_field, intensity, table, column_high, column_low)

    bundle = jnp.concatenate([back, exchanged(near, 0), exchanged(far, 1)])
    gathered = lax.all_gather(bundle, "depth")

    return pl.pallas_call(
        correction_kernel,
        out_shape=jax.ShapeDtypeStruct((2, levels, tile, width), jnp.float32),
        in_specs=[scalars()] * 8 + [resident()],
        out_specs=pl.BlockSpec(memory_space=pl.ANY),
        scratch_shapes=[
            pltpu.VMEM((2, halves, (3 * frames + 1) * reach, LANES), jnp.float32),
            pltpu.VMEM((2, halves, 3 * frames * reach, LANES), jnp.float32),
            pltpu.VMEM((2, levels, tile, width), jnp.float32),
            pltpu.SemaphoreType.DMA(()),
        ],
        compiler_params=params(24),
        interpret=INTERPRET,
        name="corrections",
    )(place, positions, angle_index, below, above, shear_rate, cosines, sines, gathered)


def solution(mesh):
    placed = (
        P(None, "depth", "lat", None),
        P(),
        P("lat", None, None),
        P(None, "depth"),
        P(),
        P("lat"),
        P("lat"),
        P("lat"),
    )
    return jax.shard_map(
        shards, mesh=mesh, in_specs=placed, out_specs=P(None, "depth", "lat", None), check_vma=False
    )
```

```python
import math

import jax
import jax.numpy as jnp
import ml_dtypes
import numpy as np
from jax import lax
from jax.experimental import pallas as pl
from jax.experimental.pallas import tpu as pltpu
from jax.sharding import PartitionSpec as P

INTERPRET = False
LANES = 128
HEAD = 16
STEPS = 128.0
TOP = 32700.0
SHIFTER = 12582912.0


def split_pair(table):
    high = table.astype(ml_dtypes.bfloat16)
    low = (table - high.astype(np.float64)).astype(ml_dtypes.bfloat16)
    return high, low


def dft_pair(length):
    index = np.arange(length, dtype=np.int64)
    theta = 2.0 * np.pi / length * (index[:, None] * index[None, :] % length)
    factor = 1.0 / math.sqrt(length)
    return np.cos(theta) * factor, np.sin(theta) * factor


def row_table(length):
    high, low = split_pair(np.concatenate(dft_pair(length), axis=0))
    return np.concatenate([high, low, high], axis=1)


def column_tables(length):
    return split_pair(np.concatenate(dft_pair(length), axis=1))


def column_code(peak):
    bounded = jnp.maximum(peak, 2.0**-100)
    return jnp.ceil(jnp.log(bounded) * (STEPS / math.log(2.0))) + 1.0


def code_gain(code):
    return TOP * jnp.exp(code * (-math.log(2.0) / STEPS))


def code_step(code):
    return jnp.exp(code * (math.log(2.0) / STEPS)) * (1.0 / TOP)


def whole(value, gain):
    return ((value * gain + SHIFTER) - SHIFTER).astype(jnp.int32)


def coded(value, gain):
    return whole(value, gain).astype(jnp.int16)


def widened(value):
    return value.astype(jnp.int32).astype(jnp.float32)


def shift_of(shear, level, total):
    return lax.shift_right_arithmetic(shear * (2 * level - total), int(math.log2(2 * total)))


def exit_kernel(
    slab,
    side,
    positions,
    angles,
    shears,
    cosines,
    sines,
    own,
    near,
    far,
    out,
    extended,
    wave,
    staged,
    sem,
):
    frames = out.shape[0]
    levels, tile = own.shape[1], own.shape[2]
    reach = tile // 2
    halves = own.shape[3] // LANES
    total = 8 * levels
    first = slab[0] * levels
    near_at = pl.multiple_of((1 - side[0]) * (reach + tile), reach)
    far_at = pl.multiple_of(side[0] * (reach + tile), reach)

    def fill(level, carry):
        for part in range(2):
            rim = pl.ds(pl.multiple_of((part * levels + level) * reach, reach), reach)
            for half in range(halves):
                lanes = slice(half * LANES, (half + 1) * LANES)
                extended[part, level, half, pl.ds(near_at, reach)] = near[rim, lanes].astype(
                    jnp.float32
                )
                extended[part, level, half, reach : reach + tile] = own[
                    part, level, :, lanes
                ].astype(jnp.float32)
                extended[part, level, half, pl.ds(far_at, reach)] = far[rim, lanes].astype(
                    jnp.float32
                )
        return carry

    lax.fori_loop(0, levels, fill, 0, unroll=True)

    def one(frame, carry):
        angle = angles[frame]
        shear = shears[angle]
        base = reach + positions[frame]
        starts = [base + shift_of(shear, first + level, total) for level in range(levels)]
        ramps = [
            (cosines[angle * levels + level], sines[angle * levels + level])
            for level in range(levels)
        ]
        for half in range(halves):
            lanes = slice(half * LANES, (half + 1) * LANES)
            peak = jnp.zeros((1, LANES), jnp.float32)
            for chunk in range(2):
                sum_real = jnp.zeros((reach, LANES), jnp.float32)
                sum_imag = jnp.zeros((reach, LANES), jnp.float32)
                for level in range(levels):
                    rows = pl.ds(starts[level] + chunk * reach, reach)
                    real = extended[0, level, half, rows]
                    imag = extended[1, level, half, rows]
                    ramp_real, ramp_imag = ramps[level]
                    sum_real = sum_real + (real * ramp_real - imag * ramp_imag)
                    sum_imag = sum_imag + (real * ramp_imag + imag * ramp_real)
                wave[0, chunk] = sum_real
                wave[1, chunk] = sum_imag
                top = jnp.maximum(jnp.abs(sum_real), jnp.abs(sum_imag))
                peak = jnp.maximum(peak, jnp.max(top, axis=0, keepdims=True))
            code = column_code(peak)
            gain = code_gain(code)
            for part in range(2):
                for chunk in range(2):
                    at = (part * 2 + chunk) * reach
                    staged[frame, at : at + reach, lanes] = coded(wave[part, chunk], gain)
            staged[frame, 4 * reach :, lanes] = (
                jnp.broadcast_to(code, (HEAD, LANES)).astype(jnp.int32).astype(jnp.int16)
            )
        pltpu.make_async_copy(staged.at[frame], out.at[frame], sem).start()
        return carry

    lax.fori_loop(0, frames, one, 0, unroll=True)
    pltpu.make_async_copy(staged, out, sem).wait()


def halves_of(value):
    high = value.astype(jnp.bfloat16)
    low = (value - high.astype(jnp.float32)).astype(jnp.bfloat16)
    return high, low


def matmul(left, right):
    return jnp.dot(left, right, preferred_element_type=jnp.float32)


def row_products(table, real, imag):
    high, low = halves_of(jnp.concatenate([real, imag], axis=1))
    both = matmul(table[...], jnp.concatenate([high, high, low], axis=0))
    rows, columns = real.shape
    return (
        both[:rows, :columns],
        both[:rows, columns:],
        both[rows:, :columns],
        both[rows:, columns:],
    )


def column_products(table_high, table_low, real, imag):
    high, low = halves_of(jnp.concatenate([real, imag], axis=0))
    both = matmul(high, table_high[...])
    both = both + matmul(high, table_low[...])
    both = both + matmul(low, table_high[...])
    rows, columns = real.shape
    return (
        both[:rows, :columns],
        both[rows:, :columns],
        both[:rows, columns:],
        both[rows:, columns:],
    )


def frame_kernel(
    slab,
    side,
    count,
    *refs,
    total,
):
    *parts, probe, intensity, row_ref, column_high, column_low, out, near_out, far_out = refs
    tile = probe.shape[1]
    reach = tile // 2
    sums_real, sums_imag = [], []
    for partials in parts:
        sum_real = jnp.zeros((tile, partials.shape[2]), jnp.float32)
        sum_imag = jnp.zeros((tile, partials.shape[2]), jnp.float32)
        for source in range(partials.shape[0]):
            step = code_step(widened(partials[source, 4 * reach :])[:1])
            sum_real = sum_real + widened(partials[source, : 2 * reach]) * step
            sum_imag = sum_imag + widened(partials[source, 2 * reach : 4 * reach]) * step
        sums_real.append(sum_real)
        sums_imag.append(sum_imag)
    sum_real = jnp.concatenate(sums_real, axis=1)
    sum_imag = jnp.concatenate(sums_imag, axis=1)
    scale = 1.0 / math.sqrt(total)
    sum_real = sum_real * scale
    sum_imag = sum_imag * scale
    probe_real = probe[0].astype(jnp.float32)
    probe_imag = probe[1].astype(jnp.float32)
    wave_real = probe_real * sum_real - probe_imag * sum_imag
    wave_imag = probe_real * sum_imag + probe_imag * sum_real

    cos_real, cos_imag, sin_real, sin_imag = row_products(row_ref, wave_real, wave_imag)
    mid_real = cos_real + sin_imag
    mid_imag = cos_imag - sin_real
    cos_real, cos_imag, sin_real, sin_imag = column_products(
        column_high, column_low, mid_real, mid_imag
    )
    far_real = cos_real + sin_imag
    far_imag = cos_imag - sin_real

    magnitude = jnp.sqrt(far_real * far_real + far_imag * far_imag)
    amplitude = jnp.sqrt(intensity[slab[0]].astype(jnp.float32))
    valid = jnp.where(slab[0] < count[0], 1.0, 0.0).astype(jnp.float32)
    factor = (amplitude / jnp.maximum(magnitude, 0.5) - 1.0) * valid
    far_real = far_real * factor
    far_imag = far_imag * factor

    cos_real, cos_imag, sin_real, sin_imag = column_products(
        column_high, column_low, far_real, far_imag
    )
    mid_real = cos_real - sin_imag
    mid_imag = cos_imag + sin_real
    cos_real, cos_imag, sin_real, sin_imag = row_products(row_ref, mid_real, mid_imag)
    update_real = cos_real - sin_imag
    update_imag = cos_imag + sin_real

    back_real = probe_real * update_real + probe_imag * update_imag
    back_imag = probe_real * update_imag - probe_imag * update_real
    peak = jnp.max(
        jnp.maximum(jnp.abs(back_real), jnp.abs(back_imag)), axis=0, keepdims=True
    )
    code = column_code(peak)
    gain = code_gain(code)
    rounded_real = whole(back_real, gain)
    rounded_imag = whole(back_imag, gain)
    head = jnp.broadcast_to(code, (HEAD, code.shape[1])).astype(jnp.int32).astype(jnp.int16)
    out[: 2 * reach] = rounded_real.astype(jnp.int16)
    out[2 * reach : 4 * reach] = rounded_imag.astype(jnp.int16)
    out[4 * reach :] = head

    even = side[0] == 0
    for part, value in enumerate((rounded_real, rounded_imag)):
        rows = slice(part * reach, (part + 1) * reach)
        near_out[rows] = jnp.where(even, value[reach:], value[:reach]).astype(jnp.int16)
        far_out[rows] = jnp.where(even, value[:reach], value[reach:]).astype(jnp.int16)
    near_out[2 * reach :] = head
    far_out[2 * reach :] = head


def correction_kernel(
    slab, side, positions, angles, below, above, shears, cosines, sines, *refs
):
    gathered, out, inner, rims, staged, sem = refs
    levels, tile = out.shape[1], out.shape[2]
    reach = tile // 2
    halves = out.shape[3] // LANES
    frames = gathered.shape[0]
    total = 8 * levels
    blank = jnp.zeros((reach, LANES), jnp.float32)
    head_at = 4 * reach
    near_at = head_at + HEAD
    far_at = near_at + 2 * reach + HEAD
    lower_at = pl.multiple_of(jnp.where(side[0] == 0, far_at, near_at), HEAD)
    upper_at = pl.multiple_of(jnp.where(side[0] == 0, near_at, far_at), HEAD)
    for part in range(2):
        for half in range(halves):
            inner[part, half, :reach] = blank

    def fill(frame, carry):
        own = pl.multiple_of(reach + frame * 3 * reach, reach)
        rim = pl.multiple_of(frame * 3 * reach, reach)
        for half in range(halves):
            lanes = slice(half * LANES, (half + 1) * LANES)

            def step_at(row):
                return code_step(widened(gathered[frame, pl.ds(row, HEAD), lanes])[:1])

            step = step_at(head_at)
            lower_step = step_at(lower_at + 2 * reach)
            upper_step = step_at(upper_at + 2 * reach)
            for part in range(2):
                at = 2 * part * reach
                inner[part, half, pl.ds(own, tile)] = (
                    widened(gathered[frame, at : at + tile, lanes]) * step
                )
                inner[part, half, pl.ds(own + tile, reach)] = blank
                at = lower_at + part * reach
                rims[part, half, pl.ds(rim, reach)] = (
                    widened(gathered[frame, pl.ds(at, reach), lanes]) * lower_step
                )
                rims[part, half, pl.ds(rim + reach, reach)] = blank
                at = upper_at + part * reach
                rims[part, half, pl.ds(rim + 2 * reach, reach)] = (
                    widened(gathered[frame, pl.ds(at, reach), lanes]) * upper_step
                )
        return carry

    lax.fori_loop(0, frames, fill, 0, unroll=True)

    def one(level, carry):
        here = slab[0] * levels + level
        starts, ramps = [], []
        for frame in range(frames):
            angle = angles[frame]
            start = positions[frame] + shift_of(shears[angle], here, total)
            starts.append((3 * frame + 1) * reach - start)
            ramps.append((cosines[angle * levels + level], sines[angle * levels + level]))
        for chunk, around in enumerate((below, above)):
            rim_starts, rim_ramps = [], []
            for frame in range(frames):
                angle = around[frames + frame]
                start = around[frame] + shift_of(shears[angle], here, total)
                if chunk == 0:
                    rim_starts.append((3 * frame + 1) * reach - jnp.maximum(start, 0))
                else:
                    rim_starts.append((3 * frame + 1) * reach - jnp.minimum(start, 0))
                rim_ramps.append((cosines[angle * levels + level], sines[angle * levels + level]))
            at = slice(chunk * reach, (chunk + 1) * reach)
            for half in range(halves):
                lanes = slice(half * LANES, (half + 1) * LANES)
                sum_real = jnp.zeros((reach, LANES), jnp.float32)
                sum_imag = jnp.zeros((reach, LANES), jnp.float32)
                for frame in range(frames):
                    for source, first, (ramp_real, ramp_imag) in (
                        (inner, starts[frame] + chunk * reach, ramps[frame]),
                        (rims, rim_starts[frame], rim_ramps[frame]),
                    ):
                        real = source[0, half, pl.ds(first, reach)]
                        imag = source[1, half, pl.ds(first, reach)]
                        sum_real = sum_real + (real * ramp_real + imag * ramp_imag)
                        sum_imag = sum_imag + (imag * ramp_real - real * ramp_imag)
                staged[0, level, at, lanes] = sum_real
                staged[1, level, at, lanes] = sum_imag
        for part in range(2):
            pltpu.make_async_copy(staged.at[part, level], out.at[part, level], sem).start()
        return carry

    lax.fori_loop(0, levels, one, 0, unroll=True)
    pltpu.make_async_copy(staged, out, sem).wait()


def scalars():
    return pl.BlockSpec(memory_space=pltpu.SMEM)


def resident():
    return pl.BlockSpec(memory_space=pltpu.VMEM)


def params(mebibytes):
    return pltpu.CompilerParams(vmem_limit_bytes=mebibytes << 20)


def exchanged(value, shift):
    count = lax.axis_size("lat")
    pairs = [(i, ((i + shift) ^ 1) - shift) for i in range(count)]
    return lax.ppermute(value, "lat", [(i, j) for i, j in pairs if 0 <= j < count])


def shards(
    object_field,
    probe_field,
    intensity,
    depth_phase,
    shear_rate,
    positions,
    angle_index,
    frame_count,
):
    levels = object_field.shape[1]
    tile = object_field.shape[2]
    width = object_field.shape[3]
    frames = positions.shape[0]
    reach = tile // 2
    halves = width // LANES
    slabs = lax.axis_size("depth")
    total = levels * slabs
    odd = lax.axis_index("lat").astype(jnp.int32) & 1
    slab = lax.axis_index("depth").astype(jnp.int32).reshape(1)
    side = odd.reshape(1)
    coded_rows = 2 * tile + HEAD

    spots = jnp.concatenate([positions, angle_index]).astype(jnp.bfloat16)
    spots = jnp.pad(spots[None], ((0, HEAD - 1), (0, width - 2 * frames)))
    rim_rows = 2 * levels * reach
    last = object_field[:, :, reach:].reshape(rim_rows, width)
    first = object_field[:, :, :reach].reshape(rim_rows, width)
    near = jnp.concatenate([jnp.where(odd == 0, last, first), spots])
    far = jnp.concatenate([jnp.where(odd == 0, first, last), spots])
    near = exchanged(near, 0)
    far = exchanged(far, 1)
    near_spots = near[rim_rows, : 2 * frames].astype(jnp.int32)
    far_spots = far[rim_rows, : 2 * frames].astype(jnp.int32)
    below = jnp.where(odd == 0, far_spots, near_spots)
    above = jnp.where(odd == 0, near_spots, far_spots)
    cosines = jnp.cos(depth_phase).reshape(-1)
    sines = jnp.sin(depth_phase).reshape(-1)

    partials = pl.pallas_call(
        exit_kernel,
        out_shape=jax.ShapeDtypeStruct((frames, coded_rows, width), jnp.int16),
        in_specs=[scalars()] * 7 + [resident()] * 3,
        out_specs=pl.BlockSpec(memory_space=pl.ANY),
        scratch_shapes=[
            pltpu.VMEM((2, levels, halves, 2 * tile, LANES), jnp.float32),
            pltpu.VMEM((2, 2, reach, LANES), jnp.float32),
            pltpu.VMEM((frames, coded_rows, width), jnp.int16),
            pltpu.SemaphoreType.DMA(()),
        ],
        compiler_params=params(16),
        interpret=INTERPRET,
        name="exit_waves",
    )(slab, side, positions, angle_index, shear_rate, cosines, sines, object_field, near, far)
    received = lax.all_to_all(partials, "depth", 0, 0)

    table = jnp.asarray(row_table(tile))
    column_high, column_low = (jnp.asarray(t) for t in column_tables(width))
    half_rows = tile + HEAD
    back, near, far = pl.pallas_call(
        lambda *refs: frame_kernel(*refs, total=total),
        out_shape=[
            jax.ShapeDtypeStruct((rows, width), jnp.int16)
            for rows in (coded_rows, half_rows, half_rows)
        ],
        in_specs=[scalars()] * 3 + [resident()] * 6,
        out_specs=[resident()] * 3,
        compiler_params=params(16),
        interpret=INTERPRET,
        name="far_field",
    )(slab, side, frame_count, received, probe_field, intensity, table, column_high, column_low)

    bundle = jnp.concatenate([back, exchanged(near, 0), exchanged(far, 1)])
    gathered = lax.all_gather(bundle, "depth")

    return pl.pallas_call(
        correction_kernel,
        out_shape=jax.ShapeDtypeStruct((2, levels, tile, width), jnp.float32),
        in_specs=[scalars()] * 9 + [resident()],
        out_specs=pl.BlockSpec(memory_space=pl.ANY),
        scratch_shapes=[
            pltpu.VMEM((2, halves, (3 * frames + 1) * reach, LANES), jnp.float32),
            pltpu.VMEM((2, halves, 3 * frames * reach, LANES), jnp.float32),
            pltpu.VMEM((2, levels, tile, width), jnp.float32),
            pltpu.SemaphoreType.DMA(()),
        ],
        compiler_params=params(24),
        interpret=INTERPRET,
        name="corrections",
    )(slab, side, positions, angle_index, below, above, shear_rate, cosines, sines, gathered)


def solution(mesh):
    placed = (
        P(None, "depth", "lat", None),
        P(),
        P("lat", None, None),
        P(None, "depth"),
        P(),
        P("lat"),
        P("lat"),
        P("lat"),
    )
    return jax.shard_map(
        shards, mesh=mesh, in_specs=placed, out_specs=P(None, "depth", "lat", None), check_vma=False
    )
```

```python
import math

import jax
import jax.numpy as jnp
import ml_dtypes
import numpy as np
from jax import lax
from jax.experimental import pallas as pl
from jax.experimental.pallas import tpu as pltpu
from jax.sharding import PartitionSpec as P

INTERPRET = False
LANES = 128
HEAD = 8
STEPS = 128.0
TOP = 32700.0
SHIFTER = 12582912.0


def split_pair(table):
    high = table.astype(ml_dtypes.bfloat16)
    low = (table - high.astype(np.float64)).astype(ml_dtypes.bfloat16)
    return high, low


def dft_pair(length):
    index = np.arange(length, dtype=np.int64)
    theta = 2.0 * np.pi / length * (index[:, None] * index[None, :] % length)
    factor = 1.0 / math.sqrt(length)
    return np.cos(theta) * factor, np.sin(theta) * factor


def row_table(length):
    high, low = split_pair(np.concatenate(dft_pair(length), axis=0))
    return np.concatenate([high, low, high], axis=1)


def column_tables(length):
    return split_pair(np.concatenate(dft_pair(length), axis=1))


def column_code(peak):
    bounded = jnp.maximum(peak, 2.0**-100)
    return jnp.ceil(jnp.log(bounded) * (STEPS / math.log(2.0))) + 1.0


def code_gain(code):
    return TOP * jnp.exp(code * (-math.log(2.0) / STEPS))


def code_step(code):
    return jnp.exp(code * (math.log(2.0) / STEPS)) * (1.0 / TOP)


def whole(value, gain):
    return ((value * gain + SHIFTER) - SHIFTER).astype(jnp.int32)


def coded(value, gain):
    return whole(value, gain).astype(jnp.int16)


def widened(value):
    return value.astype(jnp.int32).astype(jnp.float32)


def shift_of(shear, level, total):
    return lax.shift_right_arithmetic(shear * (2 * level - total), int(math.log2(2 * total)))


def exit_kernel(
    slab,
    side,
    positions,
    angles,
    shears,
    cosines,
    sines,
    own,
    near,
    far,
    out,
    extended,
    wave,
    staged,
    sem,
):
    frames = out.shape[0]
    levels, tile = own.shape[1], own.shape[2]
    reach = tile // 2
    halves = own.shape[3] // LANES
    total = 8 * levels
    first = slab[0] * levels
    near_at = pl.multiple_of((1 - side[0]) * (reach + tile), reach)
    far_at = pl.multiple_of(side[0] * (reach + tile), reach)

    def fill(level, carry):
        for part in range(2):
            rim = pl.ds(pl.multiple_of((part * levels + level) * reach, reach), reach)
            for half in range(halves):
                lanes = slice(half * LANES, (half + 1) * LANES)
                extended[part, level, half, pl.ds(near_at, reach)] = near[rim, lanes].astype(
                    jnp.float32
                )
                extended[part, level, half, reach : reach + tile] = own[
                    part, level, :, lanes
                ].astype(jnp.float32)
                extended[part, level, half, pl.ds(far_at, reach)] = far[rim, lanes].astype(
                    jnp.float32
                )
        return carry

    lax.fori_loop(0, levels, fill, 0, unroll=True)

    def one(frame, carry):
        angle = angles[frame]
        shear = shears[angle]
        base = reach + positions[frame]
        starts = [base + shift_of(shear, first + level, total) for level in range(levels)]
        ramps = [
            (cosines[angle * levels + level], sines[angle * levels + level])
            for level in range(levels)
        ]
        for half in range(halves):
            lanes = slice(half * LANES, (half + 1) * LANES)
            peak = jnp.zeros((1, LANES), jnp.float32)
            for chunk in range(2):
                sum_real = jnp.zeros((reach, LANES), jnp.float32)
                sum_imag = jnp.zeros((reach, LANES), jnp.float32)
                for level in range(levels):
                    rows = pl.ds(starts[level] + chunk * reach, reach)
                    real = extended[0, level, half, rows]
                    imag = extended[1, level, half, rows]
                    ramp_real, ramp_imag = ramps[level]
                    sum_real = sum_real + (real * ramp_real - imag * ramp_imag)
                    sum_imag = sum_imag + (real * ramp_imag + imag * ramp_real)
                wave[0, chunk] = sum_real
                wave[1, chunk] = sum_imag
                top = jnp.maximum(jnp.abs(sum_real), jnp.abs(sum_imag))
                peak = jnp.maximum(peak, jnp.max(top, axis=0, keepdims=True))
            code = column_code(peak)
            gain = code_gain(code)
            for part in range(2):
                for chunk in range(2):
                    at = (part * 2 + chunk) * reach
                    staged[frame, at : at + reach, lanes] = coded(wave[part, chunk], gain)
            staged[frame, 4 * reach :, lanes] = (
                jnp.broadcast_to(code, (HEAD, LANES)).astype(jnp.int32).astype(jnp.int16)
            )
        pltpu.make_async_copy(staged.at[frame], out.at[frame], sem).start()
        return carry

    lax.fori_loop(0, frames, one, 0, unroll=True)
    pltpu.make_async_copy(staged, out, sem).wait()


def halves_of(value):
    high = value.astype(jnp.bfloat16)
    low = (value - high.astype(jnp.float32)).astype(jnp.bfloat16)
    return high, low


def matmul(left, right):
    return jnp.dot(left, right, preferred_element_type=jnp.float32)


def row_products(table, real, imag):
    high, low = halves_of(jnp.concatenate([real, imag], axis=1))
    both = matmul(table[...], jnp.concatenate([high, high, low], axis=0))
    rows, columns = real.shape
    return (
        both[:rows, :columns],
        both[:rows, columns:],
        both[rows:, :columns],
        both[rows:, columns:],
    )


def column_products(table_high, table_low, real, imag):
    high, low = halves_of(jnp.concatenate([real, imag], axis=0))
    both = matmul(high, table_high[...])
    both = both + matmul(high, table_low[...])
    both = both + matmul(low, table_high[...])
    rows, columns = real.shape
    return (
        both[:rows, :columns],
        both[rows:, :columns],
        both[:rows, columns:],
        both[rows:, columns:],
    )


def frame_kernel(
    slab,
    side,
    count,
    *refs,
    total,
):
    *parts, probe, intensity, row_ref, column_high, column_low, out, near_out, far_out = refs
    tile = probe.shape[1]
    reach = tile // 2
    sums_real, sums_imag = [], []
    for partials in parts:
        sum_real = jnp.zeros((tile, partials.shape[2]), jnp.float32)
        sum_imag = jnp.zeros((tile, partials.shape[2]), jnp.float32)
        for source in range(partials.shape[0]):
            step = code_step(widened(partials[source, 4 * reach :])[:1])
            sum_real = sum_real + widened(partials[source, : 2 * reach]) * step
            sum_imag = sum_imag + widened(partials[source, 2 * reach : 4 * reach]) * step
        sums_real.append(sum_real)
        sums_imag.append(sum_imag)
    sum_real = jnp.concatenate(sums_real, axis=1)
    sum_imag = jnp.concatenate(sums_imag, axis=1)
    scale = 1.0 / math.sqrt(total)
    sum_real = sum_real * scale
    sum_imag = sum_imag * scale
    probe_real = probe[0].astype(jnp.float32)
    probe_imag = probe[1].astype(jnp.float32)
    wave_real = probe_real * sum_real - probe_imag * sum_imag
    wave_imag = probe_real * sum_imag + probe_imag * sum_real

    cos_real, cos_imag, sin_real, sin_imag = row_products(row_ref, wave_real, wave_imag)
    mid_real = cos_real + sin_imag
    mid_imag = cos_imag - sin_real
    cos_real, cos_imag, sin_real, sin_imag = column_products(
        column_high, column_low, mid_real, mid_imag
    )
    far_real = cos_real + sin_imag
    far_imag = cos_imag - sin_real

    magnitude = jnp.sqrt(far_real * far_real + far_imag * far_imag)
    amplitude = jnp.sqrt(intensity[slab[0]].astype(jnp.float32))
    valid = jnp.where(slab[0] < count[0], 1.0, 0.0).astype(jnp.float32)
    factor = (amplitude / jnp.maximum(magnitude, 0.5) - 1.0) * valid
    far_real = far_real * factor
    far_imag = far_imag * factor

    cos_real, cos_imag, sin_real, sin_imag = column_products(
        column_high, column_low, far_real, far_imag
    )
    mid_real = cos_real - sin_imag
    mid_imag = cos_imag + sin_real
    cos_real, cos_imag, sin_real, sin_imag = row_products(row_ref, mid_real, mid_imag)
    update_real = cos_real - sin_imag
    update_imag = cos_imag + sin_real

    back_real = probe_real * update_real + probe_imag * update_imag
    back_imag = probe_real * update_imag - probe_imag * update_real
    peak = jnp.max(
        jnp.maximum(jnp.abs(back_real), jnp.abs(back_imag)), axis=0, keepdims=True
    )
    code = column_code(peak)
    gain = code_gain(code)
    rounded_real = whole(back_real, gain)
    rounded_imag = whole(back_imag, gain)
    head = jnp.broadcast_to(code, (HEAD, code.shape[1])).astype(jnp.int32).astype(jnp.int16)
    out[: 2 * reach] = rounded_real.astype(jnp.int16)
    out[2 * reach : 4 * reach] = rounded_imag.astype(jnp.int16)
    out[4 * reach :] = head

    even = side[0] == 0
    for part, value in enumerate((rounded_real, rounded_imag)):
        rows = slice(part * reach, (part + 1) * reach)
        near_out[rows] = jnp.where(even, value[reach:], value[:reach]).astype(jnp.int16)
        far_out[rows] = jnp.where(even, value[:reach], value[reach:]).astype(jnp.int16)
    near_out[2 * reach :] = head
    far_out[2 * reach :] = head


def correction_kernel(
    slab, side, positions, angles, below, above, shears, cosines, sines, *refs
):
    gathered, out, inner, rims, staged, sem = refs
    levels, tile = out.shape[1], out.shape[2]
    reach = tile // 2
    halves = out.shape[3] // LANES
    frames = gathered.shape[0]
    total = 8 * levels
    blank = jnp.zeros((reach, LANES), jnp.float32)
    head_at = 4 * reach
    near_at = head_at + HEAD
    far_at = near_at + 2 * reach + HEAD
    lower_at = pl.multiple_of(jnp.where(side[0] == 0, far_at, near_at), HEAD)
    upper_at = pl.multiple_of(jnp.where(side[0] == 0, near_at, far_at), HEAD)
    for part in range(2):
        for half in range(halves):
            inner[part, half, :reach] = blank

    def fill(frame, carry):
        own = pl.multiple_of(reach + frame * 3 * reach, reach)
        rim = pl.multiple_of(frame * 3 * reach, reach)
        for half in range(halves):
            lanes = slice(half * LANES, (half + 1) * LANES)

            def step_at(row):
                return code_step(widened(gathered[frame, pl.ds(row, HEAD), lanes])[:1])

            step = step_at(head_at)
            lower_step = step_at(lower_at + 2 * reach)
            upper_step = step_at(upper_at + 2 * reach)
            for part in range(2):
                at = 2 * part * reach
                inner[part, half, pl.ds(own, tile)] = (
                    widened(gathered[frame, at : at + tile, lanes]) * step
                )
                inner[part, half, pl.ds(own + tile, reach)] = blank
                at = lower_at + part * reach
                rims[part, half, pl.ds(rim, reach)] = (
                    widened(gathered[frame, pl.ds(at, reach), lanes]) * lower_step
                )
                rims[part, half, pl.ds(rim + reach, reach)] = blank
                at = upper_at + part * reach
                rims[part, half, pl.ds(rim + 2 * reach, reach)] = (
                    widened(gathered[frame, pl.ds(at, reach), lanes]) * upper_step
                )
        return carry

    lax.fori_loop(0, frames, fill, 0, unroll=True)

    def one(level, carry):
        here = slab[0] * levels + level
        starts, ramps = [], []
        for frame in range(frames):
            angle = angles[frame]
            start = positions[frame] + shift_of(shears[angle], here, total)
            starts.append((3 * frame + 1) * reach - start)
            ramps.append((cosines[angle * levels + level], sines[angle * levels + level]))
        for chunk, around in enumerate((below, above)):
            rim_starts, rim_ramps = [], []
            for frame in range(frames):
                angle = around[frames + frame]
                start = around[frame] + shift_of(shears[angle], here, total)
                if chunk == 0:
                    rim_starts.append((3 * frame + 1) * reach - jnp.maximum(start, 0))
                else:
                    rim_starts.append((3 * frame + 1) * reach - jnp.minimum(start, 0))
                rim_ramps.append((cosines[angle * levels + level], sines[angle * levels + level]))
            at = slice(chunk * reach, (chunk + 1) * reach)
            for half in range(halves):
                lanes = slice(half * LANES, (half + 1) * LANES)
                sum_real = jnp.zeros((reach, LANES), jnp.float32)
                sum_imag = jnp.zeros((reach, LANES), jnp.float32)
                for frame in range(frames):
                    for source, first, (ramp_real, ramp_imag) in (
                        (inner, starts[frame] + chunk * reach, ramps[frame]),
                        (rims, rim_starts[frame], rim_ramps[frame]),
                    ):
                        real = source[0, half, pl.ds(first, reach)]
                        imag = source[1, half, pl.ds(first, reach)]
                        sum_real = sum_real + (real * ramp_real + imag * ramp_imag)
                        sum_imag = sum_imag + (imag * ramp_real - real * ramp_imag)
                staged[0, level, at, lanes] = sum_real
                staged[1, level, at, lanes] = sum_imag
        for part in range(2):
            pltpu.make_async_copy(staged.at[part, level], out.at[part, level], sem).start()
        return carry

    lax.fori_loop(0, levels, one, 0, unroll=True)
    pltpu.make_async_copy(staged, out, sem).wait()


def scalars():
    return pl.BlockSpec(memory_space=pltpu.SMEM)


def resident():
    return pl.BlockSpec(memory_space=pltpu.VMEM)


def params(mebibytes):
    return pltpu.CompilerParams(vmem_limit_bytes=mebibytes << 20)


def exchanged(value, shift):
    count = lax.axis_size("lat")
    pairs = [(i, ((i + shift) ^ 1) - shift) for i in range(count)]
    return lax.ppermute(value, "lat", [(i, j) for i, j in pairs if 0 <= j < count])


def shards(
    object_field,
    probe_field,
    intensity,
    depth_phase,
    shear_rate,
    positions,
    angle_index,
    frame_count,
):
    levels = object_field.shape[1]
    tile = object_field.shape[2]
    width = object_field.shape[3]
    frames = positions.shape[0]
    reach = tile // 2
    halves = width // LANES
    slabs = lax.axis_size("depth")
    total = levels * slabs
    odd = lax.axis_index("lat").astype(jnp.int32) & 1
    slab = lax.axis_index("depth").astype(jnp.int32).reshape(1)
    side = odd.reshape(1)
    coded_rows = 2 * tile + HEAD

    spots = jnp.concatenate([positions, angle_index]).astype(jnp.bfloat16)
    spots = jnp.pad(spots[None], ((0, HEAD - 1), (0, width - 2 * frames)))
    rim_rows = 2 * levels * reach
    last = object_field[:, :, reach:].reshape(rim_rows, width)
    first = object_field[:, :, :reach].reshape(rim_rows, width)
    near = jnp.concatenate([jnp.where(odd == 0, last, first), spots])
    far = jnp.concatenate([jnp.where(odd == 0, first, last), spots])
    near = exchanged(near, 0)
    far = exchanged(far, 1)
    near_spots = near[rim_rows, : 2 * frames].astype(jnp.int32)
    far_spots = far[rim_rows, : 2 * frames].astype(jnp.int32)
    below = jnp.where(odd == 0, far_spots, near_spots)
    above = jnp.where(odd == 0, near_spots, far_spots)
    cosines = jnp.cos(depth_phase).reshape(-1)
    sines = jnp.sin(depth_phase).reshape(-1)

    partials = pl.pallas_call(
        exit_kernel,
        out_shape=jax.ShapeDtypeStruct((frames, coded_rows, width), jnp.int16),
        in_specs=[scalars()] * 7 + [resident()] * 3,
        out_specs=pl.BlockSpec(memory_space=pl.ANY),
        scratch_shapes=[
            pltpu.VMEM((2, levels, halves, 2 * tile, LANES), jnp.float32),
            pltpu.VMEM((2, 2, reach, LANES), jnp.float32),
            pltpu.VMEM((frames, coded_rows, width), jnp.int16),
            pltpu.SemaphoreType.DMA(()),
        ],
        compiler_params=params(16),
        interpret=INTERPRET,
        name="exit_waves",
    )(slab, side, positions, angle_index, shear_rate, cosines, sines, object_field, near, far)
    received = lax.all_to_all(partials, "depth", 0, 0)

    table = jnp.asarray(row_table(tile))
    column_high, column_low = (jnp.asarray(t) for t in column_tables(width))
    half_rows = tile + HEAD
    back, near, far = pl.pallas_call(
        lambda *refs: frame_kernel(*refs, total=total),
        out_shape=[
            jax.ShapeDtypeStruct((rows, width), jnp.int16)
            for rows in (coded_rows, half_rows, half_rows)
        ],
        in_specs=[scalars()] * 3 + [resident()] * 6,
        out_specs=[resident()] * 3,
        compiler_params=params(16),
        interpret=INTERPRET,
        name="far_field",
    )(slab, side, frame_count, received, probe_field, intensity, table, column_high, column_low)

    bundle = jnp.concatenate([back, exchanged(near, 0), exchanged(far, 1)])
    gathered = lax.all_gather(bundle, "depth")

    return pl.pallas_call(
        correction_kernel,
        out_shape=jax.ShapeDtypeStruct((2, levels, tile, width), jnp.float32),
        in_specs=[scalars()] * 9 + [resident()],
        out_specs=pl.BlockSpec(memory_space=pl.ANY),
        scratch_shapes=[
            pltpu.VMEM((2, halves, (3 * frames + 1) * reach, LANES), jnp.float32),
            pltpu.VMEM((2, halves, 3 * frames * reach, LANES), jnp.float32),
            pltpu.VMEM((2, levels, tile, width), jnp.float32),
            pltpu.SemaphoreType.DMA(()),
        ],
        compiler_params=params(24),
        interpret=INTERPRET,
        name="corrections",
    )(slab, side, positions, angle_index, below, above, shear_rate, cosines, sines, gathered)


def solution(mesh):
    placed = (
        P(None, "depth", "lat", None),
        P(),
        P("lat", None, None),
        P(None, "depth"),
        P(),
        P("lat"),
        P("lat"),
        P("lat"),
    )
    return jax.shard_map(
        shards, mesh=mesh, in_specs=placed, out_specs=P(None, "depth", "lat", None), check_vma=False
    )
```

```python
import math

import jax
import jax.numpy as jnp
import ml_dtypes
import numpy as np
from jax import lax
from jax.experimental import pallas as pl
from jax.experimental.pallas import tpu as pltpu
from jax.sharding import PartitionSpec as P

INTERPRET = False
LANES = 128
HEAD = 8
STEPS = 128.0
TOP = 32700.0
SHIFTER = 12582912.0


def split_pair(table):
    high = table.astype(ml_dtypes.bfloat16)
    low = (table - high.astype(np.float64)).astype(ml_dtypes.bfloat16)
    return high, low


def dft_pair(length):
    index = np.arange(length, dtype=np.int64)
    theta = 2.0 * np.pi / length * (index[:, None] * index[None, :] % length)
    factor = 1.0 / math.sqrt(length)
    return np.cos(theta) * factor, np.sin(theta) * factor


def row_table(length):
    high, low = split_pair(np.concatenate(dft_pair(length), axis=0))
    return np.concatenate([high, low, high], axis=1)


def column_tables(length):
    return split_pair(np.concatenate(dft_pair(length), axis=1))


def column_code(peak):
    bounded = jnp.maximum(peak, 2.0**-100)
    return jnp.ceil(jnp.log(bounded) * (STEPS / math.log(2.0))) + 1.0


def code_gain(code):
    return TOP * jnp.exp(code * (-math.log(2.0) / STEPS))


def code_step(code):
    return jnp.exp(code * (math.log(2.0) / STEPS)) * (1.0 / TOP)


def whole(value, gain):
    return ((value * gain + SHIFTER) - SHIFTER).astype(jnp.int32)


def coded(value, gain):
    return whole(value, gain).astype(jnp.int16)


def widened(value):
    return value.astype(jnp.int32).astype(jnp.float32)


def shift_of(shear, level, total):
    return lax.shift_right_arithmetic(shear * (2 * level - total), int(math.log2(2 * total)))


def exit_kernel(
    slab,
    side,
    positions,
    angles,
    shears,
    cosines,
    sines,
    own,
    near,
    far,
    out,
    extended,
    wave,
    staged,
    sem,
):
    frames = out.shape[0]
    levels, tile = own.shape[1], own.shape[2]
    reach = tile // 2
    halves = own.shape[3] // LANES
    total = 8 * levels
    first = slab[0] * levels
    near_at = pl.multiple_of((1 - side[0]) * (reach + tile), reach)
    far_at = pl.multiple_of(side[0] * (reach + tile), reach)

    def fill(level, carry):
        for part in range(2):
            rim = pl.ds(pl.multiple_of((part * levels + level) * reach, reach), reach)
            for half in range(halves):
                lanes = slice(half * LANES, (half + 1) * LANES)
                extended[part, level, half, pl.ds(near_at, reach)] = near[rim, lanes].astype(
                    jnp.float32
                )
                extended[part, level, half, reach : reach + tile] = own[
                    part, level, :, lanes
                ].astype(jnp.float32)
                extended[part, level, half, pl.ds(far_at, reach)] = far[rim, lanes].astype(
                    jnp.float32
                )
        return carry

    lax.fori_loop(0, levels, fill, 0, unroll=True)

    def one(frame, carry):
        angle = angles[frame]
        shear = shears[angle]
        base = reach + positions[frame]
        starts = [base + shift_of(shear, first + level, total) for level in range(levels)]
        ramps = [
            (cosines[angle * levels + level], sines[angle * levels + level])
            for level in range(levels)
        ]
        for half in range(halves):
            lanes = slice(half * LANES, (half + 1) * LANES)
            peak = jnp.zeros((1, LANES), jnp.float32)
            for chunk in range(2):
                sum_real = jnp.zeros((reach, LANES), jnp.float32)
                sum_imag = jnp.zeros((reach, LANES), jnp.float32)
                for level in range(levels):
                    rows = pl.ds(starts[level] + chunk * reach, reach)
                    real = extended[0, level, half, rows]
                    imag = extended[1, level, half, rows]
                    ramp_real, ramp_imag = ramps[level]
                    sum_real = sum_real + (real * ramp_real - imag * ramp_imag)
                    sum_imag = sum_imag + (real * ramp_imag + imag * ramp_real)
                wave[0, chunk] = sum_real
                wave[1, chunk] = sum_imag
                top = jnp.maximum(jnp.abs(sum_real), jnp.abs(sum_imag))
                peak = jnp.maximum(peak, jnp.max(top, axis=0, keepdims=True))
            code = column_code(peak)
            gain = code_gain(code)
            for part in range(2):
                for chunk in range(2):
                    at = (part * 2 + chunk) * reach
                    staged[frame, at : at + reach, lanes] = coded(wave[part, chunk], gain)
            staged[frame, 4 * reach :, lanes] = (
                jnp.broadcast_to(code, (HEAD, LANES)).astype(jnp.int32).astype(jnp.int16)
            )
        pltpu.make_async_copy(staged.at[frame], out.at[frame], sem).start()
        return carry

    lax.fori_loop(0, frames, one, 0, unroll=True)
    pltpu.make_async_copy(staged, out, sem).wait()


def halves_of(value):
    high = value.astype(jnp.bfloat16)
    low = (value - high.astype(jnp.float32)).astype(jnp.bfloat16)
    return high, low


def matmul(left, right):
    return jnp.dot(left, right, preferred_element_type=jnp.float32)


def row_products(table, real, imag):
    high, low = halves_of(jnp.concatenate([real, imag], axis=1))
    both = matmul(table[...], jnp.concatenate([high, high, low], axis=0))
    rows, columns = real.shape
    return (
        both[:rows, :columns],
        both[:rows, columns:],
        both[rows:, :columns],
        both[rows:, columns:],
    )


def column_products(table_high, table_low, real, imag):
    high, low = halves_of(jnp.concatenate([real, imag], axis=0))
    both = matmul(high, table_high[...])
    both = both + matmul(high, table_low[...])
    both = both + matmul(low, table_high[...])
    rows, columns = real.shape
    return (
        both[:rows, :columns],
        both[rows:, :columns],
        both[:rows, columns:],
        both[rows:, columns:],
    )


def frame_kernel(
    slab,
    side,
    count,
    *refs,
    total,
):
    *parts, neighbour_spots, probe, intensity, row_ref, column_high, column_low, out, near_out, far_out = refs
    tile = probe.shape[1]
    reach = tile // 2
    sums_real, sums_imag = [], []
    for partials in parts:
        sum_real = jnp.zeros((tile, partials.shape[2]), jnp.float32)
        sum_imag = jnp.zeros((tile, partials.shape[2]), jnp.float32)
        for source in range(partials.shape[0]):
            step = code_step(widened(partials[source, 4 * reach :])[:1])
            sum_real = sum_real + widened(partials[source, : 2 * reach]) * step
            sum_imag = sum_imag + widened(partials[source, 2 * reach : 4 * reach]) * step
        sums_real.append(sum_real)
        sums_imag.append(sum_imag)
    sum_real = jnp.concatenate(sums_real, axis=1)
    sum_imag = jnp.concatenate(sums_imag, axis=1)
    scale = 1.0 / math.sqrt(total)
    sum_real = sum_real * scale
    sum_imag = sum_imag * scale
    probe_real = probe[0].astype(jnp.float32)
    probe_imag = probe[1].astype(jnp.float32)
    wave_real = probe_real * sum_real - probe_imag * sum_imag
    wave_imag = probe_real * sum_imag + probe_imag * sum_real

    cos_real, cos_imag, sin_real, sin_imag = row_products(row_ref, wave_real, wave_imag)
    mid_real = cos_real + sin_imag
    mid_imag = cos_imag - sin_real
    cos_real, cos_imag, sin_real, sin_imag = column_products(
        column_high, column_low, mid_real, mid_imag
    )
    far_real = cos_real + sin_imag
    far_imag = cos_imag - sin_real

    magnitude = jnp.sqrt(far_real * far_real + far_imag * far_imag)
    amplitude = jnp.sqrt(intensity[slab[0]].astype(jnp.float32))
    valid = jnp.where(slab[0] < count[0], 1.0, 0.0).astype(jnp.float32)
    factor = (amplitude / jnp.maximum(magnitude, 0.5) - 1.0) * valid
    far_real = far_real * factor
    far_imag = far_imag * factor

    cos_real, cos_imag, sin_real, sin_imag = column_products(
        column_high, column_low, far_real, far_imag
    )
    mid_real = cos_real - sin_imag
    mid_imag = cos_imag + sin_real
    cos_real, cos_imag, sin_real, sin_imag = row_products(row_ref, mid_real, mid_imag)
    update_real = cos_real - sin_imag
    update_imag = cos_imag + sin_real

    back_real = probe_real * update_real + probe_imag * update_imag
    back_imag = probe_real * update_imag - probe_imag * update_real
    peak = jnp.max(
        jnp.maximum(jnp.abs(back_real), jnp.abs(back_imag)), axis=0, keepdims=True
    )
    code = column_code(peak)
    gain = code_gain(code)
    rounded_real = whole(back_real, gain)
    rounded_imag = whole(back_imag, gain)
    head = jnp.broadcast_to(code, (HEAD, code.shape[1])).astype(jnp.int32).astype(jnp.int16)
    out[: 2 * reach] = rounded_real.astype(jnp.int16)
    out[2 * reach : 4 * reach] = rounded_imag.astype(jnp.int16)
    out[4 * reach :] = head

    even = side[0] == 0
    for part, value in enumerate((rounded_real, rounded_imag)):
        rows = slice(part * reach, (part + 1) * reach)
        near_out[rows] = jnp.where(even, value[reach:], value[:reach]).astype(jnp.int16)
        far_out[rows] = jnp.where(even, value[:reach], value[reach:]).astype(jnp.int16)
    top_row = lax.broadcasted_iota(jnp.int32, head.shape, 0) == 0
    spots = neighbour_spots[...].astype(jnp.int32)
    head = jnp.where(top_row, head.astype(jnp.int32), spots).astype(jnp.int16)
    near_out[2 * reach :] = head
    far_out[2 * reach :] = head


def correction_kernel(
    slab, side, positions, angles, below, above, shears, cosines, sines, *refs
):
    gathered, out, inner, rims, staged, sem = refs
    levels, tile = out.shape[1], out.shape[2]
    reach = tile // 2
    halves = out.shape[3] // LANES
    frames = gathered.shape[0]
    total = 8 * levels
    blank = jnp.zeros((reach, LANES), jnp.float32)
    head_at = 4 * reach
    near_at = head_at + HEAD
    far_at = near_at + 2 * reach + HEAD
    lower_at = pl.multiple_of(jnp.where(side[0] == 0, far_at, near_at), HEAD)
    upper_at = pl.multiple_of(jnp.where(side[0] == 0, near_at, far_at), HEAD)
    for part in range(2):
        for half in range(halves):
            inner[part, half, :reach] = blank

    def fill(frame, carry):
        own = pl.multiple_of(reach + frame * 3 * reach, reach)
        rim = pl.multiple_of(frame * 3 * reach, reach)
        for half in range(halves):
            lanes = slice(half * LANES, (half + 1) * LANES)

            def step_at(row):
                return code_step(widened(gathered[frame, pl.ds(row, HEAD), lanes])[:1])

            step = step_at(head_at)
            lower_step = step_at(lower_at + 2 * reach)
            upper_step = step_at(upper_at + 2 * reach)
            for part in range(2):
                at = 2 * part * reach
                inner[part, half, pl.ds(own, tile)] = (
                    widened(gathered[frame, at : at + tile, lanes]) * step
                )
                inner[part, half, pl.ds(own + tile, reach)] = blank
                at = lower_at + part * reach
                rims[part, half, pl.ds(rim, reach)] = (
                    widened(gathered[frame, pl.ds(at, reach), lanes]) * lower_step
                )
                rims[part, half, pl.ds(rim + reach, reach)] = blank
                at = upper_at + part * reach
                rims[part, half, pl.ds(rim + 2 * reach, reach)] = (
                    widened(gathered[frame, pl.ds(at, reach), lanes]) * upper_step
                )
        return carry

    lax.fori_loop(0, frames, fill, 0, unroll=True)

    def one(level, carry):
        here = slab[0] * levels + level
        starts, ramps = [], []
        for frame in range(frames):
            angle = angles[frame]
            start = positions[frame] + shift_of(shears[angle], here, total)
            starts.append((3 * frame + 1) * reach - start)
            ramps.append((cosines[angle * levels + level], sines[angle * levels + level]))
        for chunk, around in enumerate((below, above)):
            rim_starts, rim_ramps = [], []
            for frame in range(frames):
                angle = around[frames + frame]
                start = around[frame] + shift_of(shears[angle], here, total)
                if chunk == 0:
                    rim_starts.append((3 * frame + 1) * reach - jnp.maximum(start, 0))
                else:
                    rim_starts.append((3 * frame + 1) * reach - jnp.minimum(start, 0))
                rim_ramps.append((cosines[angle * levels + level], sines[angle * levels + level]))
            at = slice(chunk * reach, (chunk + 1) * reach)
            for half in range(halves):
                lanes = slice(half * LANES, (half + 1) * LANES)
                sum_real = jnp.zeros((reach, LANES), jnp.float32)
                sum_imag = jnp.zeros((reach, LANES), jnp.float32)
                for frame in range(frames):
                    for source, first, (ramp_real, ramp_imag) in (
                        (inner, starts[frame] + chunk * reach, ramps[frame]),
                        (rims, rim_starts[frame], rim_ramps[frame]),
                    ):
                        real = source[0, half, pl.ds(first, reach)]
                        imag = source[1, half, pl.ds(first, reach)]
                        sum_real = sum_real + (real * ramp_real + imag * ramp_imag)
                        sum_imag = sum_imag + (imag * ramp_real - real * ramp_imag)
                staged[0, level, at, lanes] = sum_real
                staged[1, level, at, lanes] = sum_imag
        for part in range(2):
            pltpu.make_async_copy(staged.at[part, level], out.at[part, level], sem).start()
        return carry

    lax.fori_loop(0, levels, one, 0, unroll=True)
    pltpu.make_async_copy(staged, out, sem).wait()


def scalars():
    return pl.BlockSpec(memory_space=pltpu.SMEM)


def resident():
    return pl.BlockSpec(memory_space=pltpu.VMEM)


def params(mebibytes):
    return pltpu.CompilerParams(vmem_limit_bytes=mebibytes << 20)


def exchanged(value, shift):
    count = lax.axis_size("lat")
    pairs = [(i, ((i + shift) ^ 1) - shift) for i in range(count)]
    return lax.ppermute(value, "lat", [(i, j) for i, j in pairs if 0 <= j < count])


def shards(
    object_field,
    probe_field,
    intensity,
    depth_phase,
    shear_rate,
    positions,
    angle_index,
    frame_count,
):
    levels = object_field.shape[1]
    tile = object_field.shape[2]
    width = object_field.shape[3]
    frames = positions.shape[0]
    reach = tile // 2
    halves = width // LANES
    slabs = lax.axis_size("depth")
    total = levels * slabs
    odd = lax.axis_index("lat").astype(jnp.int32) & 1
    slab = lax.axis_index("depth").astype(jnp.int32).reshape(1)
    side = odd.reshape(1)
    coded_rows = 2 * tile + HEAD

    spots = jnp.concatenate([positions, angle_index]).astype(jnp.int16)
    spots = jnp.pad(spots[None], ((1, HEAD - 2), (0, width - 2 * frames)))
    rim_rows = 2 * levels * reach
    last = object_field[:, :, reach:].reshape(rim_rows, width)
    first = object_field[:, :, :reach].reshape(rim_rows, width)
    near = exchanged(jnp.where(odd == 0, last, first), 0)
    far = exchanged(jnp.where(odd == 0, first, last), 1)
    cosines = jnp.cos(depth_phase).reshape(-1)
    sines = jnp.sin(depth_phase).reshape(-1)

    partials = pl.pallas_call(
        exit_kernel,
        out_shape=jax.ShapeDtypeStruct((frames, coded_rows, width), jnp.int16),
        in_specs=[scalars()] * 7 + [resident()] * 3,
        out_specs=pl.BlockSpec(memory_space=pl.ANY),
        scratch_shapes=[
            pltpu.VMEM((2, levels, halves, 2 * tile, LANES), jnp.float32),
            pltpu.VMEM((2, 2, reach, LANES), jnp.float32),
            pltpu.VMEM((frames, coded_rows, width), jnp.int16),
            pltpu.SemaphoreType.DMA(()),
        ],
        compiler_params=params(16),
        interpret=INTERPRET,
        name="exit_waves",
    )(slab, side, positions, angle_index, shear_rate, cosines, sines, object_field, near, far)
    received = lax.all_to_all(partials, "depth", 0, 0)

    table = jnp.asarray(row_table(tile))
    column_high, column_low = (jnp.asarray(t) for t in column_tables(width))
    half_rows = tile + HEAD
    back, near, far = pl.pallas_call(
        lambda *refs: frame_kernel(*refs, total=total),
        out_shape=[
            jax.ShapeDtypeStruct((rows, width), jnp.int16)
            for rows in (coded_rows, half_rows, half_rows)
        ],
        in_specs=[scalars()] * 3 + [resident()] * 7,
        out_specs=[resident()] * 3,
        compiler_params=params(16),
        interpret=INTERPRET,
        name="far_field",
    )(slab, side, frame_count, received, spots, probe_field, intensity, table, column_high, column_low)

    near = exchanged(near, 0)
    far = exchanged(far, 1)
    near_spots = near[tile + 1, : 2 * frames].astype(jnp.int32)
    far_spots = far[tile + 1, : 2 * frames].astype(jnp.int32)
    below = jnp.where(odd == 0, far_spots, near_spots)
    above = jnp.where(odd == 0, near_spots, far_spots)
    bundle = jnp.concatenate([back, near, far])
    gathered = lax.all_gather(bundle, "depth")

    return pl.pallas_call(
        correction_kernel,
        out_shape=jax.ShapeDtypeStruct((2, levels, tile, width), jnp.float32),
        in_specs=[scalars()] * 9 + [resident()],
        out_specs=pl.BlockSpec(memory_space=pl.ANY),
        scratch_shapes=[
            pltpu.VMEM((2, halves, (3 * frames + 1) * reach, LANES), jnp.float32),
            pltpu.VMEM((2, halves, 3 * frames * reach, LANES), jnp.float32),
            pltpu.VMEM((2, levels, tile, width), jnp.float32),
            pltpu.SemaphoreType.DMA(()),
        ],
        compiler_params=params(24),
        interpret=INTERPRET,
        name="corrections",
    )(slab, side, positions, angle_index, below, above, shear_rate, cosines, sines, gathered)


def solution(mesh):
    placed = (
        P(None, "depth", "lat", None),
        P(),
        P("lat", None, None),
        P(None, "depth"),
        P(),
        P("lat"),
        P("lat"),
        P("lat"),
    )
    return jax.shard_map(
        shards, mesh=mesh, in_specs=placed, out_specs=P(None, "depth", "lat", None), check_vma=False
    )
```
